32 devices in a mesh: dp: 16 (over z, y, core), tensor: 2 (over x).
Axes of the slice: x: 2, y: 2, z: 4, core: 2. Of those that a mesh axis runs over, the one named last changes fastest.
Arguments:
- residual: bfloat16 [2048, 4096], P(('dp', 'tensor')), may hold values from -6 to 6
- queries: bfloat16 [2048, 2048], P('dp', 'tensor'), may hold values from -6 to 6
- new_kv: bfloat16 [2, 2048, 2048], P(None, 'dp', 'tensor'), may hold values from -6 to 6
- kv_pool: bfloat16 [64, 2, 16, 2048], P('dp', None, None, 'tensor'), may hold values from -6 to 6
- fetch_pages: int32 [16, 16, 2], replicated, may hold values from 0 to 3
- page_owner: int32 [16, 32], P('dp'), may hold values from 0 to 7
- segment_ids: int32 [16, 128], P('dp'), may hold values from 0 to 7, never falling along the last dimension, each value on 1 to 32 neighbouring positions
- out_weight: bfloat16 [2048, 4096], P('tensor'), may hold values from -0.125 to 0.125
- out_bias: bfloat16 [4096], replicated, may hold values from -3 to 3
Outputs:
- hidden_out: bfloat16 [2048, 4096], P(('dp', 'tensor'))
- key_cache: bfloat16 [2048, 2048], P('dp', 'tensor')
The draws below stay inside these ranges and needn't reach their ends.
All inputs are finite; a program needn't handle non-finite values.
Results may differ from the reference program's by a relative error of at most 0.0055.
Values may be sent and summed in bfloat16 or wider, within the bound.
No kernel may reach another device: no remote copies, remote signals or barrier semaphores. Data moves between devices by JAX's collectives and lax.ppermute only.
A program may use at most 64 MiB of HBM per device.

```python
import math
import jax
import jax.numpy as jnp
import numpy as np
from jax import lax

D = 4096
HEADS = 16
HD = 128
ROT = 32
REQ = 8
PAGE = 16
POOL = 4
PER_PEER = 2
GROUP_TOK = 128
N_DP = 16
N_TENSOR = 2


def draw_queries(key, part):
    full_shape = (N_DP * GROUP_TOK, HEADS * HD)
    base_draw = jnp.clip(jax.random.normal(jax.random.fold_in(key, 23), full_shape, jnp.float32), -6.0, 6.0)
    return base_draw.astype(jnp.bfloat16)


def draw_new_kv(key, part):
    full_shape = (2, N_DP * GROUP_TOK, HEADS * HD)
    base_draw = jnp.clip(jax.random.normal(jax.random.fold_in(key, 33), full_shape, jnp.float32), -6.0, 6.0)
    return base_draw.astype(jnp.bfloat16)


def plant(values, own_key, low, largest):
    longest = values.shape.index(max(values.shape))
    spots = []
    for shift in (0, 1):
        where = [jax.random.randint(jax.random.fold_in(own_key, axis), (), 0, length) for axis, length in enumerate(values.shape)]
        where[longest] = (where[longest] + shift) % values.shape[longest]
        spots.append(tuple(where))
    return values.at[spots[0]].set(low).at[spots[1]].set(largest)


def steps_of(rng, extent, cuts, smallest, top_value):
    factor_of, own = 1.0, jax.random.fold_in(rng, 6)
    for axis_at, blocks in cuts:
        draws = jnp.exp(jax.random.uniform(jax.random.fold_in(own, axis_at), (blocks,), jnp.float32, smallest / len(cuts), top_value / len(cuts)))
        factor_of = factor_of * jnp.repeat(draws, extent[axis_at] // blocks).reshape([-1 if axis == axis_at else 1 for axis in range(len(extent))])
    return factor_of


def profile(number_of, total, limit, skew):
    weights = [(1 << 20) // math.isqrt(standing ** skew) + 1 for standing in range(2, number_of + 1)]
    spare, counts = total - limit - (number_of - 1), [1] * (number_of - 1)
    while spare > 0:
        free = [i for i in range(number_of - 1) if counts[i] < limit]
        mass, budget = sum([weights[i] for i in free]), spare
        for i in free:
            addition = min(limit - counts[i], max(1, budget * weights[i] // mass), spare)
            counts[i] = counts[i] + addition
            spare = spare - addition
    return np.array([limit] + counts)


def uneven_parts(key, amount, total, limit, lean):
    if amount == 2:
        one = jax.random.randint(key, (), max(1, total - limit), min(limit, total - 1) + 1)
        return jnp.stack([one, total - one])
    sizes = jnp.asarray(profile(amount, total, limit, lean), jnp.int32)
    twos = (amount - 1) // 2
    giver, receiver = sizes[1:1 + 2 * twos:2], sizes[2:2 + 2 * twos:2]
    room = jnp.minimum(giver - 1, limit - receiver)
    moved = jax.random.randint(jax.random.fold_in(key, 1), (twos,), 0, 1 << 20) % (room + 1)
    sizes = sizes.at[1:1 + 2 * twos:2].set(giver - moved).at[2:2 + 2 * twos:2].set(receiver + moved)
    return sizes[jax.random.permutation(jax.random.fold_in(key, 2), amount)]


def gaussian(own_key, dims, scale, most, shards=(), kind=jnp.bfloat16):
    loudness = steps_of(own_key, dims, shards, -0.22, 0.18) if shards else 1.0
    values = jax.random.normal(own_key, dims, jnp.float32) * scale * loudness
    return jnp.minimum(jnp.maximum(values, -most), most).astype(kind)


def setup_inputs(seed: int = 0) -> dict:
    seeds = jax.random.split(jax.random.key(seed), 10)
    return {
        "residual": gaussian(seeds[0], (N_DP * GROUP_TOK, D), 1.0, 6.0, ((0, 32),)),
        "queries": draw_queries(jax.random.fold_in(seeds[9], 71), 0),
        "new_kv": draw_new_kv(jax.random.fold_in(seeds[9], 71), 0),
        "kv_pool": gaussian(seeds[3], (N_DP * POOL, 2, PAGE, HEADS * HD), 1.0, 6.0, ((0, 16), (3, 2))),
        "fetch_pages": plant(jax.random.randint(seeds[4], (N_DP, N_DP, PER_PEER), 0, POOL), jax.random.fold_in(seeds[4], 1), 0, POOL - 1).astype(jnp.int32),
        "page_owner": plant(jax.random.randint(seeds[5], (N_DP, N_DP * PER_PEER), 0, REQ), jax.random.fold_in(seeds[5], 1), 0, REQ - 1).astype(jnp.int32),
        "segment_ids": jax.vmap(lambda own: jnp.searchsorted(jnp.cumsum(uneven_parts(own, REQ, GROUP_TOK, GROUP_TOK // 4, 2)), jnp.arange(GROUP_TOK), side="right"))(jax.random.split(seeds[6], N_DP)).reshape((N_DP, GROUP_TOK)).astype(jnp.int32),
        "out_weight": gaussian(seeds[7], (HEADS * HD, D), (HEADS * HD) ** -0.5, 0.125, ((0, 2),)),
        "out_bias": gaussian(seeds[8], (D,), 0.5, 3.0),
    }


def rotary(values, positions):
    half_rot = ROT // 2
    frequency = jnp.exp(-jnp.log(10000.0) * (2.0 * jnp.arange(half_rot, dtype=jnp.float32) / ROT))
    angles = positions.astype(jnp.float32)[:, None] * frequency[None, :]
    cosine = jnp.cos(angles)[:, None, :]
    sine_part = jnp.sin(angles)[:, None, :]
    first_half = values[..., :half_rot]
    second_half = values[..., half_rot:ROT]
    return jnp.concatenate([first_half * cosine - second_half * sine_part, second_half * cosine + first_half * sine_part, values[..., ROT:]], axis=-1)

def token_positions(segments, owners):
    number = jnp.arange(segments.shape[0], dtype=jnp.int32)
    earlier = lax.optimization_barrier(jnp.sum((segments[None, :] < segments[:, None]).astype(jnp.int32), axis=1))
    cached = PAGE * lax.optimization_barrier(jnp.sum((owners[None, :] == segments[:, None]).astype(jnp.int32), axis=1))
    return cached + number - earlier

def reference(residual, queries, new_kv, kv_pool, fetch_pages, page_owner, segment_ids, out_weight, out_bias):
    feature = HEADS * HD
    pool_pages = kv_pool.reshape(N_DP, POOL, 2, PAGE, feature)
    sources = jnp.arange(N_DP, dtype=jnp.int32)[:, None]
    weight_shards = out_weight.reshape(N_TENSOR, feature // N_TENSOR, D)
    score_scale = 1.0 / math.sqrt(HD)
    prefix_len = N_DP * PER_PEER * PAGE

    def one_group(group_data):
        resid_rows, query_rows, kv_rows, segments, owners, wanted = group_data
        positions = token_positions(segments, owners)
        rot_query = rotary(query_rows.astype(jnp.float32).reshape(GROUP_TOK, HEADS, HD), positions).astype(jnp.bfloat16)
        rot_key = rotary(kv_rows[0].astype(jnp.float32).reshape(GROUP_TOK, HEADS, HD), positions).astype(jnp.bfloat16)
        new_values = kv_rows[1].reshape(GROUP_TOK, HEADS, HD)
        fetched = pool_pages[sources, wanted]
        all_keys = jnp.concatenate([fetched[:, :, 0].reshape(prefix_len, HEADS, HD), rot_key], axis=0)
        all_values = jnp.concatenate([fetched[:, :, 1].reshape(prefix_len, HEADS, HD), new_values], axis=0)
        key_owner = jnp.repeat(owners, PAGE)
        number = jnp.arange(GROUP_TOK, dtype=jnp.int32)
        visible = jnp.concatenate([segments[:, None] == key_owner[None, :], (segments[:, None] == segments[None, :]) & (number[None, :] <= number[:, None])], axis=1)
        query_held = lax.optimization_barrier(rot_query)
        scores = jnp.einsum('qhd,khd->hqk', query_held.astype(jnp.float32), all_keys.astype(jnp.float32)) * score_scale
        scores = jnp.where(visible[None], scores, -jnp.inf)
        row_max = lax.optimization_barrier(jnp.max(scores, axis=-1, keepdims=True))
        lifted = jnp.exp(scores - row_max)
        weights_bf = (lifted / lax.optimization_barrier(jnp.sum(lifted, axis=-1, keepdims=True))).astype(jnp.bfloat16)
        weights_bf = lax.optimization_barrier(weights_bf)
        context = jnp.einsum('hqk,khd->qhd', weights_bf.astype(jnp.float32), all_values.astype(jnp.float32)).astype(jnp.bfloat16)
        context = context.reshape(GROUP_TOK, N_TENSOR, feature // N_TENSOR)
        summed = jnp.zeros((GROUP_TOK, D), jnp.float32)
        for shard_index in range(N_TENSOR):
            part_sum = jnp.dot(context[:, shard_index], weight_shards[shard_index], preferred_element_type=jnp.float32).astype(jnp.bfloat16)
            part_sum = lax.optimization_barrier(part_sum)
            summed = summed + part_sum.astype(jnp.float32)
        output = (resid_rows.astype(jnp.float32) + summed + out_bias.astype(jnp.float32)[None, :]).astype(jnp.bfloat16)
        return (output, rot_key.reshape(GROUP_TOK, feature))
    group_data = (residual.reshape(N_DP, GROUP_TOK, D), queries.reshape(N_DP, GROUP_TOK, feature), jnp.swapaxes(new_kv.reshape(2, N_DP, GROUP_TOK, feature), 0, 1), segment_ids, page_owner, fetch_pages)
    hidden_out, key_cache = lax.map(one_group, group_data)
    return (hidden_out.reshape(N_DP * GROUP_TOK, D), key_cache.reshape(N_DP * GROUP_TOK, feature))
```

```python
import functools
import math

import jax
import jax.numpy as jnp
from jax import lax
from jax.experimental import pallas as pl
from jax.experimental.pallas import tpu as pltpu
from jax.sharding import PartitionSpec as P

HD = 128
ROT = 32
LOWEST = -1e30
VMEM_LIMIT = 48 << 20


def vmem():
    return pl.BlockSpec(memory_space=pltpu.VMEM)


def smem():
    return pl.BlockSpec(memory_space=pltpu.SMEM)


def column_of(row, size):
    rows = lax.broadcasted_iota(jnp.int32, (size, size), 0)
    cols = lax.broadcasted_iota(jnp.int32, (size, size), 1)
    spread = jnp.broadcast_to(row, (size, size))
    return jnp.sum(jnp.where(rows == cols, spread, 0.0), axis=1, keepdims=True)


def rotary_kernel(page, segments_ref, owners_ref, query_ref, kv_ref, rot_query_ref, rot_key_ref):
    tokens, feature = query_ref.shape
    segments = segments_ref[...].astype(jnp.float32)
    column = column_of(segments, tokens)
    earlier = jnp.sum(jnp.where(segments < column, 1.0, 0.0), axis=1, keepdims=True)
    owners = owners_ref[...].astype(jnp.float32)
    cached = jnp.sum(jnp.where(owners == column, 1.0, 0.0), axis=1, keepdims=True)
    number = lax.broadcasted_iota(jnp.int32, (tokens, 1), 0).astype(jnp.float32)
    positions = page * cached + number - earlier
    half = ROT // 2
    lane = lax.broadcasted_iota(jnp.int32, (tokens, HD), 1)
    pair = (lane % half).astype(jnp.float32)
    angles = positions * jnp.exp(-math.log(10000.0) * (2.0 * pair / ROT))
    cosine, sine = jnp.cos(angles), jnp.sin(angles)
    keep = jnp.where(lane < ROT, cosine, 1.0)
    from_above = jnp.where(lane < half, -sine, 0.0)
    from_below = jnp.where((lane >= half) & (lane < ROT), sine, 0.0)
    for start in range(0, feature, HD):
        for source, target in ((query_ref, rot_query_ref), (kv_ref.at[0], rot_key_ref)):
            values = source[:, start : start + HD].astype(jnp.float32)
            turned = (
                values * keep
                + pltpu.roll(values, HD - half, 1) * from_above
                + pltpu.roll(values, half, 1) * from_below
            )
            target[:, start : start + HD] = turned.astype(jnp.bfloat16)


def rotate(page, segment_ids, page_owner, queries, new_kv):
    tokens, feature = queries.shape
    shape = jax.ShapeDtypeStruct((tokens, feature), jnp.bfloat16)
    return pl.pallas_call(
        functools.partial(rotary_kernel, page),
        out_shape=(shape, shape),
        grid=(1,),
        in_specs=[
            pl.BlockSpec(segment_ids.shape, lambda i: (0, 0)),
            pl.BlockSpec(page_owner.shape, lambda i: (0, 0)),
            pl.BlockSpec((tokens, feature), lambda i: (0, 0)),
            pl.BlockSpec((1, tokens, feature), lambda i: (0, 0, 0)),
        ],
        out_specs=(
            pl.BlockSpec((tokens, feature), lambda i: (0, 0)),
            pl.BlockSpec((tokens, feature), lambda i: (0, 0)),
        ),
        cost_estimate=pl.CostEstimate(
            flops=12 * tokens * feature, bytes_accessed=8 * tokens * feature, transcendentals=0
        ),
        name="rotary",
    )(segment_ids, page_owner, queries, new_kv)


def attention_kernel(
    blocks,
    per_peer,
    wanted_ref,
    owner_ref,
    source_ref,
    segments_ref,
    query_ref,
    key_ref,
    value_ref,
    *refs,
):
    block_refs = refs[:blocks]
    out_ref, keys, values = refs[blocks:]
    tokens, feature = query_ref.shape
    page = block_refs[0].shape[2]
    prefix = blocks * per_peer * page
    place = lax.broadcasted_iota(jnp.int32, (1, prefix), 1) // page
    key_owner = jnp.full((1, prefix), -1, jnp.int32)
    for index in range(blocks):
        holder = source_ref[index]
        for slot in range(per_peer):
            piece = index * per_peer + slot
            held = wanted_ref[holder * per_peer + slot]
            keys[pl.ds(piece * page, page), :] = block_refs[index][held, 0]
            values[pl.ds(piece * page, page), :] = block_refs[index][held, 1]
            key_owner = jnp.where(
                place == piece, owner_ref[holder * per_peer + slot], key_owner
            )
    segments = segments_ref[...].astype(jnp.float32)
    column = column_of(segments, tokens)
    rows = lax.broadcasted_iota(jnp.int32, (tokens, tokens), 0)
    cols = lax.broadcasted_iota(jnp.int32, (tokens, tokens), 1)
    see_new = (column == segments) & (cols <= rows)
    see_prefix = column == key_owner.astype(jnp.float32)
    factor = math.log2(math.e) / math.sqrt(HD)
    contract = (((1,), (1,)), ((), ()))
    for start in range(0, feature, HD):
        head = slice(start, start + HD)
        query = query_ref[:, head]
        new = lax.dot_general(
            query, key_ref[:, head], contract, preferred_element_type=jnp.float32
        )
        old = lax.dot_general(query, keys[:, head], contract, preferred_element_type=jnp.float32)
        new = jnp.where(see_new, new * factor, LOWEST)
        old = jnp.where(see_prefix, old * factor, LOWEST)
        top = jnp.maximum(
            jnp.max(new, axis=1, keepdims=True), jnp.max(old, axis=1, keepdims=True)
        )
        new = jnp.exp2(new - top)
        old = jnp.exp2(old - top)
        total = jnp.sum(new, axis=1, keepdims=True) + jnp.sum(old, axis=1, keepdims=True)
        mixed = jnp.dot(
            new.astype(jnp.bfloat16), value_ref[0, :, head], preferred_element_type=jnp.float32
        ) + jnp.dot(
            old.astype(jnp.bfloat16), values[:, head], preferred_element_type=jnp.float32
        )
        out_ref[:, head] = (mixed / total).astype(jnp.bfloat16)


def attend(wanted, owners, sources, segment_ids, rot_query, rot_key, new_kv, blocks, per_peer):
    tokens, feature = rot_query.shape
    prefix = len(blocks) * per_peer * blocks[0].shape[2]
    return pl.pallas_call(
        functools.partial(attention_kernel, len(blocks), per_peer),
        out_shape=jax.ShapeDtypeStruct((tokens, feature), jnp.bfloat16),
        grid=(1,),
        in_specs=[smem()] * 3
        + [vmem()] * 3
        + [pl.BlockSpec((1, tokens, feature), lambda i: (1, 0, 0))]
        + [vmem()] * len(blocks),
        out_specs=vmem(),
        scratch_shapes=[pltpu.VMEM((prefix, feature), jnp.bfloat16)] * 2,
        compiler_params=pltpu.CompilerParams(vmem_limit_bytes=VMEM_LIMIT),
        cost_estimate=pl.CostEstimate(
            flops=4 * tokens * (prefix + tokens) * feature,
            bytes_accessed=8 * prefix * feature,
            transcendentals=0,
        ),
        name="attention",
    )(wanted, owners, sources, segment_ids, rot_query, rot_key, new_kv, *blocks)


def project_kernel(peers, context_ref, weight_ref, own_ref, *send_refs):
    rows = own_ref.shape[0]
    me = lax.axis_index("tensor")
    product = jnp.dot(
        context_ref[...], weight_ref[...], preferred_element_type=jnp.float32
    ).astype(jnp.bfloat16)
    scratch = send_refs[-1]
    scratch[...] = product
    own_ref[...] = scratch[pl.ds(pl.multiple_of(me * rows, rows), rows), :]
    for shift in range(1, peers):
        other = lax.rem(me + shift, peers)
        send_refs[shift - 1][...] = scratch[pl.ds(pl.multiple_of(other * rows, rows), rows), :]


def project(context, out_weight, peers, width):
    tokens, feature = context.shape
    columns = out_weight.shape[1]
    rows = tokens // peers
    shape = jax.ShapeDtypeStruct((rows, columns), jnp.bfloat16)
    spec = pl.BlockSpec((rows, width), lambda i: (0, i))
    return pl.pallas_call(
        functools.partial(project_kernel, peers),
        out_shape=(shape,) * peers,
        grid=(columns // width,),
        in_specs=[vmem(), pl.BlockSpec((feature, width), lambda i: (0, i))],
        out_specs=(spec,) * peers,
        scratch_shapes=[pltpu.VMEM((tokens, width), jnp.bfloat16)],
        compiler_params=pltpu.CompilerParams(vmem_limit_bytes=VMEM_LIMIT),
        cost_estimate=pl.CostEstimate(
            flops=2 * tokens * feature * columns,
            bytes_accessed=2 * feature * columns,
            transcendentals=0,
        ),
        name="project",
    )(context, out_weight)


def body(
    residual, queries, new_kv, kv_pool, fetch_pages, page_owner, segment_ids, out_weight, out_bias
):
    group = lax.axis_index("dp")
    groups = lax.axis_size("dp")
    peers = lax.axis_size("tensor")
    per_peer = fetch_pages.shape[2]
    page = kv_pool.shape[2]
    planes = groups // 4

    def along(values, shift):
        pairs = [(d, (d + 4 * shift) % groups) for d in range(groups)]
        return lax.ppermute(values, "dp", pairs)

    def across(values):
        return lax.ppermute(values, "dp", [(d, d ^ 2) for d in range(groups)])

    def beside(values):
        return lax.ppermute(values, "dp", [(d, d ^ 1) for d in range(groups)])

    found = [(kv_pool, group)]
    up = down = kv_pool
    for step in range(1, planes // 2 + 1):
        up = along(up, 1)
        found.append((up, (group - 4 * step) % groups))
        if 2 * step < planes:
            down = along(down, -1)
            found.append((down, (group + 4 * step) % groups))
    found += [(across(values), holder ^ 2) for values, holder in found]
    found += [(beside(values), holder ^ 1) for values, holder in found]
    blocks = [values for values, _ in found]
    sources = jnp.stack([holder for _, holder in found]).astype(jnp.int32)

    wanted = lax.dynamic_index_in_dim(fetch_pages, group, axis=0, keepdims=False).reshape(-1)
    rot_query, rot_key = rotate(page, segment_ids, page_owner, queries, new_kv)
    context = attend(
        wanted,
        page_owner.reshape(-1),
        sources,
        segment_ids,
        rot_query,
        rot_key,
        new_kv,
        blocks,
        per_peer,
    )
    own, *sends = project(context, out_weight, peers, 512)
    summed = residual.astype(jnp.float32) + own.astype(jnp.float32)
    for shift, values in enumerate(sends, 1):
        pairs = [(t, (t + shift) % peers) for t in range(peers)]
        summed = summed + lax.ppermute(values, "tensor", pairs).astype(jnp.float32)
    hidden = (summed + out_bias.astype(jnp.float32)[None, :]).astype(jnp.bfloat16)
    return (hidden, rot_key)


def solution(mesh):
    return jax.shard_map(
        body,
        mesh=mesh,
        in_specs=(
            P(("dp", "tensor"), None),
            P("dp", "tensor"),
            P(None, "dp", "tensor"),
            P("dp", None, None, "tensor"),
            P(),
            P("dp", None),
            P("dp", None),
            P("tensor", None),
            P(),
        ),
        out_specs=(P(("dp", "tensor"), None), P("dp", "tensor")),
        check_vma=False,
    )
```

```python
import functools
import math

import jax
import jax.numpy as jnp
from jax import lax
from jax.experimental import pallas as pl
from jax.experimental.pallas import tpu as pltpu
from jax.sharding import PartitionSpec as P

HD = 128
ROT = 32
LOWEST = -1e30
VMEM_LIMIT = 24 << 20
LATE_LIMIT = 24 << 20
ROTARY_LIMIT = 60 << 20


def vmem():
    return pl.BlockSpec(memory_space=pltpu.VMEM)


def smem():
    return pl.BlockSpec(memory_space=pltpu.SMEM)


def column_of(row, size):
    rows = lax.broadcasted_iota(jnp.int32, (size, size), 0)
    cols = lax.broadcasted_iota(jnp.int32, (size, size), 1)
    spread = jnp.broadcast_to(row, (size, size))
    return jnp.sum(jnp.where(rows == cols, spread, 0.0), axis=1, keepdims=True)


def rotary_kernel(
    page,
    segments_ref,
    owners_ref,
    query_ref,
    kv_ref,
    all_kv_ref,
    pool_ref,
    column_ref,
    rot_query_ref,
    rot_key_ref,
    value_ref,
    held_ref,
    cache_ref,
    done,
):
    copies = [
        pltpu.make_async_copy(all_kv_ref.at[1], value_ref, done.at[0]),
        pltpu.make_async_copy(pool_ref, held_ref, done.at[1]),
    ]
    for copy in copies:
        copy.start()
    tokens, feature = query_ref.shape
    segments = segments_ref[...].astype(jnp.float32)
    column = column_of(segments, tokens)
    column_ref[...] = jnp.broadcast_to(column, column_ref.shape)
    earlier = jnp.sum(jnp.where(segments < column, 1.0, 0.0), axis=1, keepdims=True)
    owners = owners_ref[...].astype(jnp.float32)
    cached = jnp.sum(jnp.where(owners == column, 1.0, 0.0), axis=1, keepdims=True)
    number = lax.broadcasted_iota(jnp.int32, (tokens, 1), 0).astype(jnp.float32)
    positions = page * cached + number - earlier
    half = ROT // 2
    lane = lax.broadcasted_iota(jnp.int32, (tokens, HD), 1)
    pair = (lane % half).astype(jnp.float32)
    angles = positions * jnp.exp(-math.log(10000.0) * (2.0 * pair / ROT))
    cosine, sine = jnp.cos(angles), jnp.sin(angles)
    keep = jnp.where(lane < ROT, cosine, 1.0)
    from_above = jnp.where(lane < half, -sine, 0.0)
    from_below = jnp.where((lane >= half) & (lane < ROT), sine, 0.0)
    for start in range(0, feature, HD):
        for source, target in ((kv_ref.at[0], rot_key_ref), (query_ref, rot_query_ref)):
            values = source[:, start : start + HD].astype(jnp.float32)
            turned = (
                values * keep
                + pltpu.roll(values, HD - half, 1) * from_above
                + pltpu.roll(values, half, 1) * from_below
            )
            target[:, start : start + HD] = turned.astype(jnp.bfloat16)
    copies.append(pltpu.make_async_copy(rot_key_ref, cache_ref, done.at[2]))
    copies[-1].start()
    for copy in copies:
        copy.wait()


def anywhere():
    return pl.BlockSpec(memory_space=pltpu.HBM)


def cheap():
    return pl.CostEstimate(flops=1, bytes_accessed=1, transcendentals=0)


def rotate(page, segment_ids, page_owner, queries, new_kv, kv_pool):
    tokens, feature = queries.shape
    shape = jax.ShapeDtypeStruct((tokens, feature), jnp.bfloat16)
    return pl.pallas_call(
        functools.partial(rotary_kernel, page),
        out_shape=(
            jax.ShapeDtypeStruct((tokens, HD), jnp.float32),
            shape,
            shape,
            shape,
            jax.ShapeDtypeStruct(kv_pool.shape, jnp.bfloat16),
            shape,
        ),
        grid=(1,),
        in_specs=[
            pl.BlockSpec(segment_ids.shape, lambda i: (0, 0)),
            pl.BlockSpec(page_owner.shape, lambda i: (0, 0)),
            pl.BlockSpec((tokens, feature), lambda i: (0, 0)),
            pl.BlockSpec((1, tokens, feature), lambda i: (0, 0, 0)),
            anywhere(),
            anywhere(),
        ],
        out_specs=(vmem(),) * 5 + (anywhere(),),
        scratch_shapes=[pltpu.SemaphoreType.DMA((3,))],
        compiler_params=params(ROTARY_LIMIT),
        cost_estimate=cheap(),
        name="rotary",
    )(segment_ids, page_owner, queries, new_kv, new_kv, kv_pool)


def stage_kernel(source_ref, target_ref, done):
    pieces = done.shape[0]
    rows = source_ref.shape[0] // pieces
    copies = []
    for piece in range(pieces):
        part = pl.ds(piece * rows, rows)
        copies.append(
            pltpu.make_async_copy(source_ref.at[part], target_ref.at[part], done.at[piece])
        )
        copies[-1].start()
    for copy in copies:
        copy.wait()


def stage(values):
    return pl.pallas_call(
        stage_kernel,
        out_shape=jax.ShapeDtypeStruct(values.shape, values.dtype),
        in_specs=[pl.BlockSpec(memory_space=pl.ANY)],
        out_specs=vmem(),
        scratch_shapes=[pltpu.SemaphoreType.DMA((8,))],
        compiler_params=params(),
        cost_estimate=cheap(),
        name="stage",
    )(values)


def gather_pages(blocks, refs, per_peer, table_ref, keys, values):
    group = lax.axis_index("dp")
    groups = lax.axis_size("dp")
    page = refs[0].shape[2]
    length = len(blocks) * per_peer * page
    place = lax.broadcasted_iota(jnp.int32, (1, length), 1) // page
    key_owner = jnp.full((1, length), -1, jnp.int32)
    used = 0
    for index, (shift, flip, cuts) in enumerate(blocks):
        holder = lax.rem(group + (4 * shift) % groups, groups) ^ flip
        parts = refs[used : used + len(cuts)]
        used += len(cuts)
        for slot in range(per_peer):
            piece = index * per_peer + slot
            held = table_ref[holder * per_peer + slot]
            rows = pl.ds(piece * page, page)
            for part, low in zip(parts, cuts):
                count = part.shape[0]

                def take(part=part, low=low, count=count):
                    at = jnp.clip(held - low, 0, count - 1)
                    keys[rows, :] = part[at, 0]
                    values[rows, :] = part[at, 1]

                if len(cuts) == 1:
                    take()
                else:
                    pl.when((held >= low) & (held < low + count))(take)
            key_owner = jnp.where(
                place == piece, table_ref[(groups + holder) * per_peer + slot], key_owner
            )
    return key_owner.astype(jnp.float32)


FACTOR = math.log2(math.e) / math.sqrt(HD)
CONTRACT = (((1,), (1,)), ((), ()))


def scores_of(query, keys, seen):
    scores = lax.dot_general(query, keys, CONTRACT, preferred_element_type=jnp.float32)
    return jnp.where(seen, scores * FACTOR, LOWEST)


def weigh(weights, values):
    return jnp.dot(weights.astype(jnp.bfloat16), values, preferred_element_type=jnp.float32)


def early_kernel(
    blocks, per_peer, table_ref, segments_ref, column_ref, query_ref, key_ref, value_ref, *refs
):
    *block_refs, mixed_ref, stats_ref, keys, values = refs
    tokens, feature = query_ref.shape
    key_owner = gather_pages(blocks, block_refs, per_peer, table_ref, keys, values)
    segments = segments_ref[...].astype(jnp.float32)
    column = column_ref[:, :1]
    rows = lax.broadcasted_iota(jnp.int32, (tokens, tokens), 0)
    cols = lax.broadcasted_iota(jnp.int32, (tokens, tokens), 1)
    see_new = (column == segments) & (cols <= rows)
    see_old = column == key_owner
    lane = lax.broadcasted_iota(jnp.int32, (tokens, HD), 1)
    tops = totals = jnp.zeros((tokens, HD), jnp.float32)
    for number, start in enumerate(range(0, feature, HD)):
        head = slice(start, start + HD)
        query = query_ref[:, head]
        new = scores_of(query, key_ref[:, head], see_new)
        old = scores_of(query, keys[:, head], see_old)
        top = jnp.maximum(
            jnp.max(new, axis=1, keepdims=True), jnp.max(old, axis=1, keepdims=True)
        )
        new = jnp.exp2(new - top)
        old = jnp.exp2(old - top)
        total = jnp.sum(new, axis=1, keepdims=True) + jnp.sum(old, axis=1, keepdims=True)
        mixed_ref[:, head] = weigh(new, value_ref[:, head]) + weigh(old, values[:, head])
        tops = jnp.where(lane == number, top, tops)
        totals = jnp.where(lane == number, total, totals)
    stats_ref[:, :HD] = tops
    stats_ref[:, HD:] = totals


def late_kernel(
    blocks,
    per_peer,
    peers,
    table_ref,
    column_ref,
    query_ref,
    mixed_ref,
    stats_ref,
    weight_ref,
    *refs,
):
    count = sum(len(cuts) for _, _, cuts in blocks)
    block_refs = refs[:count]
    own_ref, *send_refs = refs[count : count + peers]
    keys, values, context_ref, product = refs[count + peers :]
    tokens, feature = query_ref.shape
    key_owner = gather_pages(blocks, block_refs, per_peer, table_ref, keys, values)
    seen = column_ref[:, :1] == key_owner
    for number, start in enumerate(range(0, feature, HD)):
        head = slice(start, start + HD)
        scores = scores_of(query_ref[:, head], keys[:, head], seen)
        before = stats_ref[:, number : number + 1]
        top = jnp.maximum(before, jnp.max(scores, axis=1, keepdims=True))
        weights = jnp.exp2(scores - top)
        fade = jnp.exp2(before - top)
        total = stats_ref[:, HD + number : HD + number + 1] * fade + jnp.sum(
            weights, axis=1, keepdims=True
        )
        mixed = mixed_ref[:, head] * fade + weigh(weights, values[:, head])
        context_ref[:, head] = (mixed / total).astype(jnp.bfloat16)
    project_rows(peers, context_ref, weight_ref, product, own_ref, send_refs)


def project_rows(peers, context_ref, weight_ref, product, own_ref, send_refs):
    rows, width = own_ref.shape
    me = lax.axis_index("tensor")
    step = min(512, width)
    for start in range(0, width, step):
        product[:, start : start + step] = jnp.dot(
            context_ref[...],
            weight_ref[:, start : start + step],
            preferred_element_type=jnp.float32,
        ).astype(jnp.bfloat16)
    own_ref[...] = product[pl.ds(pl.multiple_of(me * rows, rows), rows), :]
    for shift in range(1, peers):
        other = lax.rem(me + shift, peers)
        send_refs[shift - 1][...] = product[pl.ds(pl.multiple_of(other * rows, rows), rows), :]


def shares(tokens, peers, width):
    return (jax.ShapeDtypeStruct((tokens // peers, width), jnp.bfloat16),) * peers


def params(limit=VMEM_LIMIT):
    return pltpu.CompilerParams(vmem_limit_bytes=limit)


def attend_early(layout, table, segment_ids, column, rot_query, rot_key, value, parts, per_peer):
    tokens, feature = rot_query.shape
    prefix = len(layout) * per_peer * parts[0].shape[2]
    return pl.pallas_call(
        functools.partial(early_kernel, layout, per_peer),
        out_shape=(
            jax.ShapeDtypeStruct((tokens, feature), jnp.float32),
            jax.ShapeDtypeStruct((tokens, 2 * HD), jnp.float32),
        ),
        grid=(1,),
        in_specs=[smem()] + [vmem()] * (5 + len(parts)),
        out_specs=(vmem(), vmem()),
        scratch_shapes=[pltpu.VMEM((prefix, feature), jnp.bfloat16)] * 2,
        compiler_params=params(),
        cost_estimate=cheap(),
        name="early",
    )(table, segment_ids, column, rot_query, rot_key, value, *parts)


def attend_late(
    layout, table, column, rot_query, mixed, stats, weight, parts, per_peer, peers
):
    tokens, feature = rot_query.shape
    prefix = len(layout) * per_peer * parts[0].shape[2]
    return pl.pallas_call(
        functools.partial(late_kernel, layout, per_peer, peers),
        out_shape=shares(tokens, peers, weight.shape[1]),
        grid=(1,),
        in_specs=[smem()] + [vmem()] * (5 + len(parts)),
        out_specs=(vmem(),) * peers,
        scratch_shapes=[pltpu.VMEM((prefix, feature), jnp.bfloat16)] * 2
        + [
            pltpu.VMEM((tokens, feature), jnp.bfloat16),
            pltpu.VMEM((tokens, weight.shape[1]), jnp.bfloat16),
        ],
        compiler_params=params(LATE_LIMIT),
        cost_estimate=cheap(),
        name="late",
    )(table, column, rot_query, mixed, stats, weight, *parts)


def body(
    residual, queries, new_kv, kv_pool, fetch_pages, page_owner, segment_ids, out_weight, out_bias
):
    group = lax.axis_index("dp")
    groups = lax.axis_size("dp")
    peers = lax.axis_size("tensor")
    per_peer = fetch_pages.shape[2]
    page = kv_pool.shape[2]
    planes = groups // 4
    reach = planes // 2

    def along(values, shift):
        pairs = [(d, (d + 4 * shift) % groups) for d in range(groups)]
        return lax.ppermute(values, "dp", pairs)

    def across(values):
        return lax.ppermute(values, "dp", [(d, d ^ 2) for d in range(groups)])

    def beside(values):
        return lax.ppermute(values, "dp", [(d, d ^ 1) for d in range(groups)])

    wanted = lax.dynamic_index_in_dim(fetch_pages, group, axis=0, keepdims=False).reshape(-1)
    table = jnp.concatenate([wanted, page_owner.reshape(-1)])
    after = lax.optimization_barrier
    ups = {0: kv_pool, 1: along(kv_pool, 1)}
    over = {0: across(kv_pool)}
    column, rot_query, rot_key, value, pool, key_cache = rotate(
        page, segment_ids, page_owner, queries, new_kv, kv_pool
    )
    later, column = after((kv_pool, column))
    ups[-1] = along(later, -1)
    ups[1], column = after((ups[1], column))
    for step in range(2, reach):
        ups[step] = along(ups[step - 1], 1)
        ups[-step] = along(ups[1 - step], -1)
    ups[reach] = along(ups[reach - 1], 1)
    first, over[0], out_weight = after((ups[1], over[0], out_weight))
    over[1] = across(first)
    weight = stage(out_weight)
    ups[-1], weight, table = after((ups[-1], weight, table))
    for step in range(2, reach):
        over[step] = across(ups[step])
    for step in range(1, reach):
        over[-step] = across(ups[-step])
    crossed, ups[reach] = after((over[reach - 1], ups[reach]))
    far = along(crossed, 1)

    early = [(-s, 0, v) for s, v in ups.items() if s] + [(0, 0, pool)]
    early += [(-s, 2, v) for s, v in over.items()]
    layout, parts = [], []
    last = min(over)
    for shift, flip, values in early:
        if values is not over[last]:
            layout += [(shift, flip, (0,)), (shift, flip ^ 1, (0,))]
            parts += [values, beside(kv_pool if values is pool else values)]
    mixed, stats = attend_early(
        layout, table, segment_ids, column, rot_query, rot_key, value, parts, per_peer
    )
    near, mixed = after((over[last], mixed))
    far, mixed = after((far, mixed))
    layout = [(-last, 2, (0,)), (-last, 3, (0,)), (-reach, 2, (0,)), (-reach, 3, (0,))]
    parts = [near, beside(near), far, beside(far)]
    own, *sends = attend_late(
        layout, table, column, rot_query, mixed, stats, weight, parts, per_peer, peers
    )
    summed = residual.astype(jnp.float32) + own.astype(jnp.float32)
    for shift, values in enumerate(sends, 1):
        pairs = [(t, (t + shift) % peers) for t in range(peers)]
        summed = summed + lax.ppermute(values, "tensor", pairs).astype(jnp.float32)
    hidden = (summed + out_bias.astype(jnp.float32)[None, :]).astype(jnp.bfloat16)
    return (hidden, key_cache)


def solution(mesh):
    return jax.shard_map(
        body,
        mesh=mesh,
        in_specs=(
            P(("dp", "tensor"), None),
            P("dp", "tensor"),
            P(None, "dp", "tensor"),
            P("dp", None, None, "tensor"),
            P(),
            P("dp", None),
            P("dp", None),
            P("tensor", None),
            P(),
        ),
        out_specs=(P(("dp", "tensor"), None), P("dp", "tensor")),
        check_vma=False,
    )
```

```python
import functools
import math

import jax
import jax.numpy as jnp
from jax import lax
from jax.experimental import pallas as pl
from jax.experimental.pallas import tpu as pltpu
from jax.sharding import PartitionSpec as P

HD = 128
ROT = 32
LOWEST = -1e30
VMEM_LIMIT = 24 << 20
LATE_LIMIT = 24 << 20
ROTARY_LIMIT = 60 << 20


def vmem():
    return pl.BlockSpec(memory_space=pltpu.VMEM)


def smem():
    return pl.BlockSpec(memory_space=pltpu.SMEM)


def column_of(row, size):
    rows = lax.broadcasted_iota(jnp.int32, (size, size), 0)
    cols = lax.broadcasted_iota(jnp.int32, (size, size), 1)
    spread = jnp.broadcast_to(row, (size, size))
    return jnp.sum(jnp.where(rows == cols, spread, 0.0), axis=1, keepdims=True)


def rotary_kernel(
    page,
    segments_ref,
    owners_ref,
    query_ref,
    kv_ref,
    all_kv_ref,
    pool_ref,
    column_ref,
    rot_query_ref,
    rot_key_ref,
    value_ref,
    held_ref,
    cache_ref,
    done,
):
    copies = [
        pltpu.make_async_copy(all_kv_ref.at[1], value_ref, done.at[0]),
        pltpu.make_async_copy(pool_ref, held_ref, done.at[1]),
    ]
    for copy in copies:
        copy.start()
    tokens, feature = query_ref.shape
    segments = segments_ref[...].astype(jnp.float32)
    column = column_of(segments, tokens)
    column_ref[...] = jnp.broadcast_to(column, column_ref.shape)
    earlier = jnp.sum(jnp.where(segments < column, 1.0, 0.0), axis=1, keepdims=True)
    owners = owners_ref[...].astype(jnp.float32)
    cached = jnp.sum(jnp.where(owners == column, 1.0, 0.0), axis=1, keepdims=True)
    number = lax.broadcasted_iota(jnp.int32, (tokens, 1), 0).astype(jnp.float32)
    positions = page * cached + number - earlier
    half = ROT // 2
    lane = lax.broadcasted_iota(jnp.int32, (tokens, HD), 1)
    pair = (lane % half).astype(jnp.float32)
    angles = positions * jnp.exp(-math.log(10000.0) * (2.0 * pair / ROT))
    cosine, sine = jnp.cos(angles), jnp.sin(angles)
    keep = jnp.where(lane < ROT, cosine, 1.0)
    from_above = jnp.where(lane < half, -sine, 0.0)
    from_below = jnp.where((lane >= half) & (lane < ROT), sine, 0.0)
    for start in range(0, feature, HD):
        for source, target in ((kv_ref.at[0], rot_key_ref), (query_ref, rot_query_ref)):
            values = source[:, start : start + HD].astype(jnp.float32)
            turned = (
                values * keep
                + pltpu.roll(values, HD - half, 1) * from_above
                + pltpu.roll(values, half, 1) * from_below
            )
            target[:, start : start + HD] = turned.astype(jnp.bfloat16)
    copies.append(pltpu.make_async_copy(rot_key_ref, cache_ref, done.at[2]))
    copies[-1].start()
    for copy in copies:
        copy.wait()


def anywhere():
    return pl.BlockSpec(memory_space=pltpu.HBM)


def cheap():
    return pl.CostEstimate(flops=1, bytes_accessed=1, transcendentals=0)


def rotate(page, segment_ids, page_owner, queries, new_kv, kv_pool):
    tokens, feature = queries.shape
    shape = jax.ShapeDtypeStruct((tokens, feature), jnp.bfloat16)
    return pl.pallas_call(
        functools.partial(rotary_kernel, page),
        out_shape=(
            jax.ShapeDtypeStruct((tokens, HD), jnp.float32),
            shape,
            shape,
            shape,
            jax.ShapeDtypeStruct(kv_pool.shape, jnp.bfloat16),
            shape,
        ),
        grid=(1,),
        in_specs=[
            pl.BlockSpec(segment_ids.shape, lambda i: (0, 0)),
            pl.BlockSpec(page_owner.shape, lambda i: (0, 0)),
            pl.BlockSpec((tokens, feature), lambda i: (0, 0)),
            pl.BlockSpec((1, tokens, feature), lambda i: (0, 0, 0)),
            anywhere(),
            anywhere(),
        ],
        out_specs=(vmem(),) * 5 + (anywhere(),),
        scratch_shapes=[pltpu.SemaphoreType.DMA((3,))],
        compiler_params=params(ROTARY_LIMIT),
        cost_estimate=cheap(),
        name="rotary",
    )(segment_ids, page_owner, queries, new_kv, new_kv, kv_pool)


def stage_kernel(source_ref, target_ref, done):
    pieces = done.shape[0]
    rows = source_ref.shape[0] // pieces
    copies = []
    for piece in range(pieces):
        part = pl.ds(piece * rows, rows)
        copies.append(
            pltpu.make_async_copy(source_ref.at[part], target_ref.at[part], done.at[piece])
        )
        copies[-1].start()
    for copy in copies:
        copy.wait()


def stage(values):
    return pl.pallas_call(
        stage_kernel,
        out_shape=jax.ShapeDtypeStruct(values.shape, values.dtype),
        in_specs=[pl.BlockSpec(memory_space=pl.ANY)],
        out_specs=vmem(),
        scratch_shapes=[pltpu.SemaphoreType.DMA((8,))],
        compiler_params=params(),
        cost_estimate=cheap(),
        name="stage",
    )(values)


def gather_pages(blocks, refs, per_peer, table_ref, keys, values):
    group = lax.axis_index("dp")
    groups = lax.axis_size("dp")
    page = refs[0].shape[2]
    length = len(blocks) * per_peer * page
    place = lax.broadcasted_iota(jnp.int32, (1, length), 1) // page
    key_owner = jnp.full((1, length), -1, jnp.int32)
    used = 0
    for index, (shift, flip, cuts) in enumerate(blocks):
        holder = lax.rem(group + (4 * shift) % groups, groups) ^ flip
        parts = refs[used : used + len(cuts)]
        used += len(cuts)
        for slot in range(per_peer):
            piece = index * per_peer + slot
            held = table_ref[holder * per_peer + slot]
            rows = pl.ds(piece * page, page)
            for part, low in zip(parts, cuts):
                count = part.shape[0]

                def take(part=part, low=low, count=count):
                    at = jnp.clip(held - low, 0, count - 1)
                    keys[rows, :] = part[at, 0]
                    values[rows, :] = part[at, 1]

                if len(cuts) == 1:
                    take()
                else:
                    pl.when((held >= low) & (held < low + count))(take)
            key_owner = jnp.where(
                place == piece, table_ref[(groups + holder) * per_peer + slot], key_owner
            )
    return key_owner.astype(jnp.float32)


FACTOR = math.log2(math.e) / math.sqrt(HD)
CONTRACT = (((1,), (1,)), ((), ()))


def scores_of(query, keys, seen):
    scores = lax.dot_general(query, keys, CONTRACT, preferred_element_type=jnp.float32)
    return jnp.where(seen, scores * FACTOR, LOWEST)


def weigh(weights, values):
    return jnp.dot(weights.astype(jnp.bfloat16), values, preferred_element_type=jnp.float32)


def early_kernel(
    blocks, per_peer, table_ref, segments_ref, column_ref, query_ref, key_ref, value_ref, *refs
):
    *block_refs, mixed_ref, stats_ref, keys, values = refs
    tokens, feature = query_ref.shape
    key_owner = gather_pages(blocks, block_refs, per_peer, table_ref, keys, values)
    segments = segments_ref[...].astype(jnp.float32)
    column = column_ref[:, :1]
    rows = lax.broadcasted_iota(jnp.int32, (tokens, tokens), 0)
    cols = lax.broadcasted_iota(jnp.int32, (tokens, tokens), 1)
    see_new = (column == segments) & (cols <= rows)
    see_old = column == key_owner
    lane = lax.broadcasted_iota(jnp.int32, (tokens, HD), 1)
    heads = [slice(start, start + HD) for start in range(0, feature, HD)]
    new = [scores_of(query_ref[:, head], key_ref[:, head], see_new) for head in heads]
    old = [scores_of(query_ref[:, head], keys[:, head], see_old) for head in heads]
    peaks = [
        jnp.maximum(jnp.max(a, axis=1, keepdims=True), jnp.max(b, axis=1, keepdims=True))
        for a, b in zip(new, old)
    ]
    new = [jnp.exp2(a - top) for a, top in zip(new, peaks)]
    old = [jnp.exp2(b - top) for b, top in zip(old, peaks)]
    tops = totals = jnp.zeros((tokens, HD), jnp.float32)
    for number, head in enumerate(heads):
        total = jnp.sum(new[number], axis=1, keepdims=True) + jnp.sum(
            old[number], axis=1, keepdims=True
        )
        mixed_ref[:, head] = weigh(new[number], value_ref[:, head]) + weigh(
            old[number], values[:, head]
        )
        tops = jnp.where(lane == number, peaks[number], tops)
        totals = jnp.where(lane == number, total, totals)
    stats_ref[:, :HD] = tops
    stats_ref[:, HD:] = totals


def late_kernel(
    blocks,
    per_peer,
    peers,
    table_ref,
    column_ref,
    query_ref,
    mixed_ref,
    stats_ref,
    weight_ref,
    *refs,
):
    count = sum(len(cuts) for _, _, cuts in blocks)
    block_refs = refs[:count]
    context_ref, own_ref, *send_refs = refs[count : count + 1 + peers]
    keys, values, product = refs[count + 1 + peers :]
    tokens, feature = query_ref.shape
    key_owner = gather_pages(blocks, block_refs, per_peer, table_ref, keys, values)
    seen = column_ref[:, :1] == key_owner
    heads = [slice(start, start + HD) for start in range(0, feature, HD)]
    scores = [scores_of(query_ref[:, head], keys[:, head], seen) for head in heads]
    before = [stats_ref[:, number : number + 1] for number in range(len(heads))]
    tops = [
        jnp.maximum(old, jnp.max(new, axis=1, keepdims=True)) for old, new in zip(before, scores)
    ]
    weights = [jnp.exp2(new - top) for new, top in zip(scores, tops)]
    fades = [jnp.exp2(old - top) for old, top in zip(before, tops)]
    added = [weigh(part, values[:, head]) for part, head in zip(weights, heads)]
    for number, head in enumerate(heads):
        total = stats_ref[:, HD + number : HD + number + 1] * fades[number] + jnp.sum(
            weights[number], axis=1, keepdims=True
        )
        mixed = mixed_ref[:, head] * fades[number] + added[number]
        context_ref[:, head] = (mixed * pl.reciprocal(total)).astype(jnp.bfloat16)
    project_rows(peers, 0, context_ref, weight_ref, product, own_ref, send_refs)


def project_rows(peers, first, context_ref, weight_ref, product, own_ref, send_refs):
    rows, width = own_ref.shape
    me = lax.axis_index("tensor")
    step = 256
    for start in range(0, width, step):
        product[:, start : start + step] = jnp.dot(
            context_ref[...],
            weight_ref[:, first + start : first + start + step],
            preferred_element_type=jnp.float32,
        ).astype(jnp.bfloat16)
    own_ref[...] = product[pl.ds(pl.multiple_of(me * rows, rows), rows), :]
    for shift in range(1, peers):
        other = lax.rem(me + shift, peers)
        send_refs[shift - 1][...] = product[pl.ds(pl.multiple_of(other * rows, rows), rows), :]


def shares(tokens, peers, width):
    return (jax.ShapeDtypeStruct((tokens // peers, width), jnp.bfloat16),) * peers


def params(limit=VMEM_LIMIT):
    return pltpu.CompilerParams(vmem_limit_bytes=limit)


def attend_early(layout, table, segment_ids, column, rot_query, rot_key, value, parts, per_peer):
    tokens, feature = rot_query.shape
    prefix = len(layout) * per_peer * parts[0].shape[2]
    return pl.pallas_call(
        functools.partial(early_kernel, layout, per_peer),
        out_shape=(
            jax.ShapeDtypeStruct((tokens, feature), jnp.float32),
            jax.ShapeDtypeStruct((tokens, 2 * HD), jnp.float32),
        ),
        grid=(1,),
        in_specs=[smem()] + [vmem()] * (5 + len(parts)),
        out_specs=(vmem(), vmem()),
        scratch_shapes=[pltpu.VMEM((prefix, feature), jnp.bfloat16)] * 2,
        compiler_params=params(),
        cost_estimate=cheap(),
        name="early",
    )(table, segment_ids, column, rot_query, rot_key, value, *parts)


def attend_late(
    layout, table, column, rot_query, mixed, stats, weight, parts, per_peer, peers, width
):
    tokens, feature = rot_query.shape
    prefix = len(layout) * per_peer * parts[0].shape[2]
    return pl.pallas_call(
        functools.partial(late_kernel, layout, per_peer, peers),
        out_shape=(jax.ShapeDtypeStruct((tokens, feature), jnp.bfloat16),)
        + shares(tokens, peers, width),
        grid=(1,),
        in_specs=[smem()] + [vmem()] * (5 + len(parts)),
        out_specs=(vmem(),) * (1 + peers),
        scratch_shapes=[pltpu.VMEM((prefix, feature), jnp.bfloat16)] * 2
        + [pltpu.VMEM((tokens, width), jnp.bfloat16)],
        compiler_params=params(LATE_LIMIT),
        cost_estimate=cheap(),
        name="late",
    )(table, column, rot_query, mixed, stats, weight, *parts)


def project_kernel(peers, first, context_ref, weight_ref, own_ref, *refs):
    *send_refs, product = refs
    project_rows(peers, first, context_ref, weight_ref, product, own_ref, send_refs)


def project(context, weight, peers, first, width):
    tokens, feature = context.shape
    return pl.pallas_call(
        functools.partial(project_kernel, peers, first),
        out_shape=shares(tokens, peers, width),
        in_specs=[vmem()] * 2,
        out_specs=(vmem(),) * peers,
        scratch_shapes=[pltpu.VMEM((tokens, width), jnp.bfloat16)],
        compiler_params=params(),
        cost_estimate=cheap(),
        name="project",
    )(context, weight)


def base_kernel(residual_ref, bias_ref, *refs):
    *own_refs, base_ref = refs
    start = 0
    for own_ref in own_refs:
        columns = slice(start, start + own_ref.shape[1])
        start += own_ref.shape[1]
        base_ref[:, columns] = (
            residual_ref[:, columns].astype(jnp.float32)
            + own_ref[...].astype(jnp.float32)
            + bias_ref[:, columns].astype(jnp.float32)
        )


def base_of(residual, bias, owns):
    return pl.pallas_call(
        base_kernel,
        out_shape=jax.ShapeDtypeStruct(residual.shape, jnp.float32),
        in_specs=[vmem()] * (2 + len(owns)),
        out_specs=vmem(),
        compiler_params=params(),
        cost_estimate=cheap(),
        name="base",
    )(residual, bias, *owns)


def finish_kernel(first, count, base_ref, *refs):
    received = refs[:count]
    hidden_ref, rounded, done = refs[-3:]
    width = rounded.shape[1]
    step = 256
    copies = []
    for piece in range(width // step):
        start = piece * step
        total = base_ref[:, first + start : first + start + step]
        for part in received:
            total = total + part[:, start : start + step].astype(jnp.float32)
        rounded[:, start : start + step] = total.astype(jnp.bfloat16)
        copies.append(
            pltpu.make_async_copy(
                rounded.at[:, start : start + step],
                hidden_ref.at[:, first + start : first + start + step],
                done.at[piece],
            )
        )
        copies[-1].start()
    for copy in copies:
        copy.wait()


def finish(base, received, first, hidden):
    rows, width = received[0].shape
    before = [] if hidden is None else [hidden]
    return pl.pallas_call(
        functools.partial(finish_kernel, first, len(received)),
        out_shape=jax.ShapeDtypeStruct(base.shape, jnp.bfloat16),
        in_specs=[vmem()] * (1 + len(received)) + [anywhere()] * len(before),
        out_specs=anywhere(),
        scratch_shapes=[
            pltpu.VMEM((rows, width), jnp.bfloat16),
            pltpu.SemaphoreType.DMA((width // 256,)),
        ],
        input_output_aliases={1 + len(received): 0} if before else {},
        compiler_params=params(),
        cost_estimate=cheap(),
        name="finish",
    )(base, *received, *before)


def body(
    residual, queries, new_kv, kv_pool, fetch_pages, page_owner, segment_ids, out_weight, out_bias
):
    group = lax.axis_index("dp")
    groups = lax.axis_size("dp")
    peers = lax.axis_size("tensor")
    per_peer = fetch_pages.shape[2]
    page = kv_pool.shape[2]
    planes = groups // 4
    reach = planes // 2

    def along(values, shift):
        pairs = [(d, (d + 4 * shift) % groups) for d in range(groups)]
        return lax.ppermute(values, "dp", pairs)

    def across(values):
        return lax.ppermute(values, "dp", [(d, d ^ 2) for d in range(groups)])

    def beside(values):
        return lax.ppermute(values, "dp", [(d, d ^ 1) for d in range(groups)])

    wanted = lax.dynamic_index_in_dim(fetch_pages, group, axis=0, keepdims=False).reshape(-1)
    table = jnp.concatenate([wanted, page_owner.reshape(-1)])
    wide = out_weight.shape[1] // 16
    widths = (6 * wide, 5 * wide, 5 * wide)
    after = lax.optimization_barrier
    ups = {0: kv_pool, 1: along(kv_pool, 1)}
    over = {0: across(kv_pool)}
    column, rot_query, rot_key, value, pool, key_cache = rotate(page, segment_ids, page_owner, queries, new_kv, kv_pool)
    later, column = after((kv_pool, column))
    ups[-1] = along(later, -1)
    ups[1], column = after((ups[1], column))
    for step in range(2, reach):
        ups[step] = along(ups[step - 1], 1)
        ups[-step] = along(ups[1 - step], -1)
    ups[reach] = along(ups[reach - 1], 1)
    first, out_weight = after((ups[1], out_weight))
    first, over[0] = after((first, over[0]))
    over[1] = across(first)
    weight = stage(out_weight)
    ups[-1], weight, table = after((ups[-1], weight, table))
    for step in range(2, reach):
        over[step] = across(ups[step])
    for step in range(1, reach):
        over[-step] = across(ups[-step])
    last = min(over)
    crossed, near = over[reach - 1], over[last]
    crossed, ups[reach] = after((crossed, ups[reach]))

    layout, parts, rest = [], [], []
    for flip, found in ((0, ups), (2, over)):
        for shift, values in found.items():
            if (flip, shift) in ((0, reach), (2, reach - 1)):
                rest.append((shift, flip, values))
            elif (flip, shift) != (2, last):
                layout += [(-shift, flip, (0,)), (-shift, flip ^ 1, (0,))]
                parts += [pool if values is kv_pool else values, beside(values)]
    mixed, stats = attend_early(
        layout, table, segment_ids, column, rot_query, rot_key, value, parts, per_peer
    )
    far = along(crossed, 1)
    near, mixed = after((near, mixed))
    far, mixed = after((far, mixed))
    rest += [(last, 2, near), (reach, 2, far)]
    layout, parts = [], []
    for shift, flip, values in rest:
        layout += [(-shift, flip, (0,)), (-shift, flip ^ 1, (0,))]
        parts += [values, beside(values)]
    context, *share = attend_late(
        layout, table, column, rot_query, mixed, stats, weight, parts, per_peer, peers, widths[0]
    )
    owns, received = [share[0]], []
    start = 0
    for number, width in enumerate(widths):
        pieces = []
        for shift, values in enumerate(share[1:], 1):
            pairs = [(t, (t + shift) % peers) for t in range(peers)]
            pieces.append(lax.ppermute(values, "tensor", pairs))
        received.append(pieces)
        start += width
        if number + 1 < len(widths):
            share = project(context, weight, peers, start, widths[number + 1])
            owns.append(share[0])
    base = base_of(residual, out_bias.reshape(1, -1), owns)
    hidden, start = None, 0
    for width, pieces in zip(widths, received):
        hidden = finish(base, pieces, start, hidden)
        start += width
    return (hidden, key_cache)


def solution(mesh):
    return jax.shard_map(
        body,
        mesh=mesh,
        in_specs=(
            P(("dp", "tensor"), None),
            P("dp", "tensor"),
            P(None, "dp", "tensor"),
            P("dp", None, None, "tensor"),
            P(),
            P("dp", None),
            P("dp", None),
            P("tensor", None),
            P(),
        ),
        out_specs=(P(("dp", "tensor"), None), P("dp", "tensor")),
        check_vma=False,
    )
```

```python
import functools
import math

import jax
import jax.numpy as jnp
from jax import lax
from jax.experimental import pallas as pl
from jax.experimental.pallas import tpu as pltpu
from jax.sharding import PartitionSpec as P

HD = 128
ROT = 32
LOWEST = -1e30
VMEM_LIMIT = 24 << 20
LATE_LIMIT = 24 << 20
ROTARY_LIMIT = 60 << 20


def vmem():
    return pl.BlockSpec(memory_space=pltpu.VMEM)


def smem():
    return pl.BlockSpec(memory_space=pltpu.SMEM)


def column_of(row, size):
    rows = lax.broadcasted_iota(jnp.int32, (size, size), 0)
    cols = lax.broadcasted_iota(jnp.int32, (size, size), 1)
    spread = jnp.broadcast_to(row, (size, size))
    return jnp.sum(jnp.where(rows == cols, spread, 0.0), axis=1, keepdims=True)


def rotary_kernel(
    page,
    segments_ref,
    owners_ref,
    query_ref,
    kv_ref,
    all_kv_ref,
    pool_ref,
    column_ref,
    rot_query_ref,
    rot_key_ref,
    value_ref,
    held_ref,
    cache_ref,
    done,
):
    copies = [
        pltpu.make_async_copy(all_kv_ref.at[1], value_ref, done.at[0]),
        pltpu.make_async_copy(pool_ref, held_ref, done.at[1]),
    ]
    for copy in copies:
        copy.start()
    tokens, feature = query_ref.shape
    segments = segments_ref[...].astype(jnp.float32)
    column = column_of(segments, tokens)
    column_ref[...] = jnp.broadcast_to(column, column_ref.shape)
    earlier = jnp.sum(jnp.where(segments < column, 1.0, 0.0), axis=1, keepdims=True)
    owners = owners_ref[...].astype(jnp.float32)
    cached = jnp.sum(jnp.where(owners == column, 1.0, 0.0), axis=1, keepdims=True)
    number = lax.broadcasted_iota(jnp.int32, (tokens, 1), 0).astype(jnp.float32)
    positions = page * cached + number - earlier
    half = ROT // 2
    lane = lax.broadcasted_iota(jnp.int32, (tokens, HD), 1)
    pair = (lane % half).astype(jnp.float32)
    angles = positions * jnp.exp(-math.log(10000.0) * (2.0 * pair / ROT))
    cosine, sine = jnp.cos(angles), jnp.sin(angles)
    keep = jnp.where(lane < ROT, cosine, 1.0)
    from_above = jnp.where(lane < half, -sine, 0.0)
    from_below = jnp.where((lane >= half) & (lane < ROT), sine, 0.0)
    for start in range(0, feature, HD):
        for source, target in ((kv_ref.at[0], rot_key_ref), (query_ref, rot_query_ref)):
            values = source[:, start : start + HD].astype(jnp.float32)
            turned = (
                values * keep
                + pltpu.roll(values, HD - half, 1) * from_above
                + pltpu.roll(values, half, 1) * from_below
            )
            target[:, start : start + HD] = turned.astype(jnp.bfloat16)
    copies.append(pltpu.make_async_copy(rot_key_ref, cache_ref, done.at[2]))
    copies[-1].start()
    for copy in copies:
        copy.wait()


def anywhere():
    return pl.BlockSpec(memory_space=pltpu.HBM)


def cheap():
    return pl.CostEstimate(flops=1, bytes_accessed=1, transcendentals=0)


def rotate(page, segment_ids, page_owner, queries, new_kv, kv_pool):
    tokens, feature = queries.shape
    shape = jax.ShapeDtypeStruct((tokens, feature), jnp.bfloat16)
    return pl.pallas_call(
        functools.partial(rotary_kernel, page),
        out_shape=(
            jax.ShapeDtypeStruct((tokens, HD), jnp.float32),
            shape,
            shape,
            shape,
            jax.ShapeDtypeStruct(kv_pool.shape, jnp.bfloat16),
            shape,
        ),
        grid=(1,),
        in_specs=[
            pl.BlockSpec(segment_ids.shape, lambda i: (0, 0)),
            pl.BlockSpec(page_owner.shape, lambda i: (0, 0)),
            pl.BlockSpec((tokens, feature), lambda i: (0, 0)),
            pl.BlockSpec((1, tokens, feature), lambda i: (0, 0, 0)),
            anywhere(),
            anywhere(),
        ],
        out_specs=(vmem(),) * 5 + (anywhere(),),
        scratch_shapes=[pltpu.SemaphoreType.DMA((3,))],
        compiler_params=params(ROTARY_LIMIT),
        cost_estimate=cheap(),
        name="rotary",
    )(segment_ids, page_owner, queries, new_kv, new_kv, kv_pool)


def stage_kernel(source_ref, target_ref, done):
    pieces = done.shape[0]
    rows = source_ref.shape[0] // pieces
    copies = []
    for piece in range(pieces):
        part = pl.ds(piece * rows, rows)
        copies.append(
            pltpu.make_async_copy(source_ref.at[part], target_ref.at[part], done.at[piece])
        )
        copies[-1].start()
    for copy in copies:
        copy.wait()


def stage(values):
    return pl.pallas_call(
        stage_kernel,
        out_shape=jax.ShapeDtypeStruct(values.shape, values.dtype),
        in_specs=[pl.BlockSpec(memory_space=pl.ANY)],
        out_specs=vmem(),
        scratch_shapes=[pltpu.SemaphoreType.DMA((8,))],
        compiler_params=params(),
        cost_estimate=cheap(),
        name="stage",
    )(values)


def gather_pages(blocks, refs, per_peer, table_ref, keys, values):
    group = lax.axis_index("dp")
    groups = lax.axis_size("dp")
    page = refs[0].shape[2]
    length = len(blocks) * per_peer * page
    place = lax.broadcasted_iota(jnp.int32, (1, length), 1) // page
    key_owner = jnp.full((1, length), -1, jnp.int32)
    used = 0
    for index, (shift, flip, cuts) in enumerate(blocks):
        holder = lax.rem(group + (4 * shift) % groups, groups) ^ flip
        parts = refs[used : used + len(cuts)]
        used += len(cuts)
        for slot in range(per_peer):
            piece = index * per_peer + slot
            held = table_ref[holder * per_peer + slot]
            rows = pl.ds(piece * page, page)
            for part, low in zip(parts, cuts):
                count = part.shape[0]

                def take(part=part, low=low, count=count):
                    at = jnp.clip(held - low, 0, count - 1)
                    keys[rows, :] = part[at, 0]
                    values[rows, :] = part[at, 1]

                if len(cuts) == 1:
                    take()
                else:
                    pl.when((held >= low) & (held < low + count))(take)
            key_owner = jnp.where(
                place == piece, table_ref[(groups + holder) * per_peer + slot], key_owner
            )
    return key_owner.astype(jnp.float32)


FACTOR = math.log2(math.e) / math.sqrt(HD)
CONTRACT = (((1,), (1,)), ((), ()))


def scores_of(query, keys, seen):
    scores = lax.dot_general(query, keys, CONTRACT, preferred_element_type=jnp.float32)
    return jnp.where(seen, scores * FACTOR, LOWEST)


def weigh(weights, values):
    both = jnp.concatenate([values, jnp.ones_like(values)], axis=1)
    return jnp.dot(weights.astype(jnp.bfloat16), both, preferred_element_type=jnp.float32)


def early_kernel(
    blocks, per_peer, table_ref, segments_ref, column_ref, query_ref, key_ref, value_ref, *refs
):
    *block_refs, mixed_ref, tops_ref, keys, values = refs
    tokens, feature = query_ref.shape
    key_owner = gather_pages(blocks, block_refs, per_peer, table_ref, keys, values)
    segments = segments_ref[...].astype(jnp.float32)
    column = column_ref[:, :1]
    rows = lax.broadcasted_iota(jnp.int32, (tokens, tokens), 0)
    cols = lax.broadcasted_iota(jnp.int32, (tokens, tokens), 1)
    see_new = (column == segments) & (cols <= rows)
    see_old = column == key_owner
    heads = [slice(start, start + HD) for start in range(0, feature, HD)]
    new = [scores_of(query_ref[:, head], key_ref[:, head], see_new) for head in heads]
    old = [scores_of(query_ref[:, head], keys[:, head], see_old) for head in heads]
    peaks = [
        jnp.maximum(jnp.max(a, axis=1, keepdims=True), jnp.max(b, axis=1, keepdims=True))
        for a, b in zip(new, old)
    ]
    new = [jnp.exp2(a - top) for a, top in zip(new, peaks)]
    old = [jnp.exp2(b - top) for b, top in zip(old, peaks)]
    for number, head in enumerate(heads):
        pair = slice(2 * head.start, 2 * head.stop)
        mixed_ref[:, pair] = weigh(new[number], value_ref[:, head]) + weigh(
            old[number], values[:, head]
        )
        tops_ref[:, head] = jnp.broadcast_to(peaks[number], (tokens, HD))


def late_kernel(
    blocks,
    per_peer,
    peers,
    table_ref,
    column_ref,
    query_ref,
    mixed_ref,
    tops_ref,
    weight_ref,
    *refs,
):
    count = sum(len(cuts) for _, _, cuts in blocks)
    block_refs = refs[:count]
    context_ref, own_ref, *send_refs = refs[count : count + 1 + peers]
    keys, values, product = refs[count + 1 + peers :]
    tokens, feature = query_ref.shape
    key_owner = gather_pages(blocks, block_refs, per_peer, table_ref, keys, values)
    seen = column_ref[:, :1] == key_owner
    heads = [slice(start, start + HD) for start in range(0, feature, HD)]
    scores = [scores_of(query_ref[:, head], keys[:, head], seen) for head in heads]
    before = [tops_ref[:, head] for head in heads]
    tops = [
        jnp.maximum(old, jnp.max(new, axis=1, keepdims=True)) for old, new in zip(before, scores)
    ]
    repeat = scores[0].shape[1] // HD
    weights = [
        jnp.exp2(new - jnp.concatenate([top] * repeat, axis=1)) for new, top in zip(scores, tops)
    ]
    fades = [jnp.exp2(old - top) for old, top in zip(before, tops)]
    added = [weigh(part, values[:, head]) for part, head in zip(weights, heads)]
    for number, head in enumerate(heads):
        pair = 2 * head.start
        total = mixed_ref[:, pair + HD : pair + 2 * HD] * fades[number] + added[number][:, HD:]
        mixed = mixed_ref[:, pair : pair + HD] * fades[number] + added[number][:, :HD]
        context_ref[:, head] = (mixed / total).astype(jnp.bfloat16)
    project_rows(peers, 0, context_ref, weight_ref, product, own_ref, send_refs)


def project_rows(peers, first, context_ref, weight_ref, product, own_ref, send_refs):
    rows, width = own_ref.shape
    me = lax.axis_index("tensor")
    step = 256
    for start in range(0, width, step):
        product[:, start : start + step] = jnp.dot(
            context_ref[...],
            weight_ref[:, first + start : first + start + step],
            preferred_element_type=jnp.float32,
        ).astype(jnp.bfloat16)
    own_ref[...] = product[pl.ds(pl.multiple_of(me * rows, rows), rows), :]
    for shift in range(1, peers):
        other = lax.rem(me + shift, peers)
        send_refs[shift - 1][...] = product[pl.ds(pl.multiple_of(other * rows, rows), rows), :]


def shares(tokens, peers, width):
    return (jax.ShapeDtypeStruct((tokens // peers, width), jnp.bfloat16),) * peers


def params(limit=VMEM_LIMIT):
    return pltpu.CompilerParams(vmem_limit_bytes=limit)


def attend_early(layout, table, segment_ids, column, rot_query, rot_key, value, parts, per_peer):
    tokens, feature = rot_query.shape
    prefix = len(layout) * per_peer * parts[0].shape[2]
    return pl.pallas_call(
        functools.partial(early_kernel, layout, per_peer),
        out_shape=(
            jax.ShapeDtypeStruct((tokens, 2 * feature), jnp.float32),
            jax.ShapeDtypeStruct((tokens, feature), jnp.float32),
        ),
        grid=(1,),
        in_specs=[smem()] + [vmem()] * (5 + len(parts)),
        out_specs=(vmem(), vmem()),
        scratch_shapes=[pltpu.VMEM((prefix, feature), jnp.bfloat16)] * 2,
        compiler_params=params(),
        cost_estimate=cheap(),
        name="early",
    )(table, segment_ids, column, rot_query, rot_key, value, *parts)


def attend_late(
    layout, table, column, rot_query, mixed, tops, weight, parts, per_peer, peers, width
):
    tokens, feature = rot_query.shape
    prefix = len(layout) * per_peer * parts[0].shape[2]
    return pl.pallas_call(
        functools.partial(late_kernel, layout, per_peer, peers),
        out_shape=(jax.ShapeDtypeStruct((tokens, feature), jnp.bfloat16),)
        + shares(tokens, peers, width),
        grid=(1,),
        in_specs=[smem()] + [vmem()] * (5 + len(parts)),
        out_specs=(vmem(),) * (1 + peers),
        scratch_shapes=[pltpu.VMEM((prefix, feature), jnp.bfloat16)] * 2
        + [pltpu.VMEM((tokens, width), jnp.bfloat16)],
        compiler_params=params(LATE_LIMIT),
        cost_estimate=cheap(),
        name="late",
    )(table, column, rot_query, mixed, tops, weight, *parts)


def project_kernel(peers, first, context_ref, weight_ref, own_ref, *refs):
    *send_refs, product = refs
    project_rows(peers, first, context_ref, weight_ref, product, own_ref, send_refs)


def project(context, weight, peers, first, width):
    tokens, feature = context.shape
    return pl.pallas_call(
        functools.partial(project_kernel, peers, first),
        out_shape=shares(tokens, peers, width),
        in_specs=[vmem()] * 2,
        out_specs=(vmem(),) * peers,
        scratch_shapes=[pltpu.VMEM((tokens, width), jnp.bfloat16)],
        compiler_params=params(),
        cost_estimate=cheap(),
        name="project",
    )(context, weight)


def base_kernel(residual_ref, bias_ref, *refs):
    *own_refs, base_ref = refs
    start = 0
    for own_ref in own_refs:
        columns = slice(start, start + own_ref.shape[1])
        start += own_ref.shape[1]
        base_ref[:, columns] = (
            residual_ref[:, columns].astype(jnp.float32)
            + own_ref[...].astype(jnp.float32)
            + bias_ref[:, columns].astype(jnp.float32)
        )


def base_of(residual, bias, owns):
    return pl.pallas_call(
        base_kernel,
        out_shape=jax.ShapeDtypeStruct(residual.shape, jnp.float32),
        in_specs=[vmem()] * (2 + len(owns)),
        out_specs=vmem(),
        compiler_params=params(),
        cost_estimate=cheap(),
        name="base",
    )(residual, bias, *owns)


def finish_kernel(first, count, base_ref, *refs):
    received = refs[:count]
    hidden_ref, rounded, done = refs[-3:]
    width = rounded.shape[1]
    step = 256
    copies = []
    for piece in range(width // step):
        start = piece * step
        total = base_ref[:, first + start : first + start + step]
        for part in received:
            total = total + part[:, start : start + step].astype(jnp.float32)
        rounded[:, start : start + step] = total.astype(jnp.bfloat16)
        copies.append(
            pltpu.make_async_copy(
                rounded.at[:, start : start + step],
                hidden_ref.at[:, first + start : first + start + step],
                done.at[piece],
            )
        )
        copies[-1].start()
    for copy in copies:
        copy.wait()


def finish(base, received, first, hidden):
    rows, width = received[0].shape
    before = [] if hidden is None else [hidden]
    return pl.pallas_call(
        functools.partial(finish_kernel, first, len(received)),
        out_shape=jax.ShapeDtypeStruct(base.shape, jnp.bfloat16),
        in_specs=[vmem()] * (1 + len(received)) + [anywhere()] * len(before),
        out_specs=anywhere(),
        scratch_shapes=[
            pltpu.VMEM((rows, width), jnp.bfloat16),
            pltpu.SemaphoreType.DMA((width // 256,)),
        ],
        input_output_aliases={1 + len(received): 0} if before else {},
        compiler_params=params(),
        cost_estimate=cheap(),
        name="finish",
    )(base, *received, *before)


def body(
    residual, queries, new_kv, kv_pool, fetch_pages, page_owner, segment_ids, out_weight, out_bias
):
    group = lax.axis_index("dp")
    groups = lax.axis_size("dp")
    peers = lax.axis_size("tensor")
    per_peer = fetch_pages.shape[2]
    page = kv_pool.shape[2]
    planes = groups // 4
    reach = planes // 2

    def along(values, shift):
        pairs = [(d, (d + 4 * shift) % groups) for d in range(groups)]
        return lax.ppermute(values, "dp", pairs)

    def across(values):
        return lax.ppermute(values, "dp", [(d, d ^ 2) for d in range(groups)])

    def beside(values):
        return lax.ppermute(values, "dp", [(d, d ^ 1) for d in range(groups)])

    wanted = lax.dynamic_index_in_dim(fetch_pages, group, axis=0, keepdims=False).reshape(-1)
    table = jnp.concatenate([wanted, page_owner.reshape(-1)])
    wide = out_weight.shape[1] // 16
    widths = (6 * wide, 5 * wide, 5 * wide)
    after = lax.optimization_barrier
    ups = {0: kv_pool, 1: along(kv_pool, 1), -1: along(kv_pool, -1)}
    over = {0: across(kv_pool)}
    column, rot_query, rot_key, value, pool, key_cache = rotate(page, segment_ids, page_owner, queries, new_kv, kv_pool)
    ups[1], column = after((ups[1], column))
    for step in range(2, reach):
        ups[step] = along(ups[step - 1], 1)
        ups[-step] = along(ups[1 - step], -1)
    ups[reach] = along(ups[reach - 1], 1)
    first, over[0], out_weight = after((ups[1], over[0], out_weight))
    over[1] = across(first)
    weight = stage(out_weight)
    ups[-1], weight, table = after((ups[-1], weight, table))
    for step in range(2, reach):
        over[step] = across(ups[step])
    for step in range(1, reach):
        over[-step] = across(ups[-step])
    last = min(over)
    crossed, near = over[reach - 1], over[last]
    crossed, ups[reach] = after((crossed, ups[reach]))

    layout, parts, rest = [], [], []
    for flip, found in ((0, ups), (2, over)):
        for shift, values in found.items():
            if (flip, shift) in ((0, reach), (2, reach - 1)):
                rest.append((shift, flip, values))
            elif (flip, shift) != (2, last):
                layout += [(-shift, flip, (0,)), (-shift, flip ^ 1, (0,))]
                parts += [pool if values is kv_pool else values, beside(values)]
    mixed, tops = attend_early(
        layout, table, segment_ids, column, rot_query, rot_key, value, parts, per_peer
    )
    far = along(crossed, 1)
    near, mixed = after((near, mixed))
    far, mixed = after((far, mixed))
    rest += [(last, 2, near), (reach, 2, far)]
    layout, parts = [], []
    for shift, flip, values in rest:
        layout += [(-shift, flip, (0,)), (-shift, flip ^ 1, (0,))]
        parts += [values, beside(values)]
    context, *share = attend_late(
        layout, table, column, rot_query, mixed, tops, weight, parts, per_peer, peers, widths[0]
    )
    owns, received = [share[0]], []
    start = 0
    for number, width in enumerate(widths):
        pieces = []
        for shift, values in enumerate(share[1:], 1):
            pairs = [(t, (t + shift) % peers) for t in range(peers)]
            pieces.append(lax.ppermute(values, "tensor", pairs))
        received.append(pieces)
        start += width
        if number + 1 < len(widths):
            share = project(context, weight, peers, start, widths[number + 1])
            owns.append(share[0])
    base = base_of(residual, out_bias.reshape(1, -1), owns)
    hidden, start = None, 0
    for width, pieces in zip(widths, received):
        hidden = finish(base, pieces, start, hidden)
        start += width
    return (hidden, key_cache)


def solution(mesh):
    return jax.shard_map(
        body,
        mesh=mesh,
        in_specs=(
            P(("dp", "tensor"), None),
            P("dp", "tensor"),
            P(None, "dp", "tensor"),
            P("dp", None, None, "tensor"),
            P(),
            P("dp", None),
            P("dp", None),
            P("tensor", None),
            P(),
        ),
        out_specs=(P(("dp", "tensor"), None), P("dp", "tensor")),
        check_vma=False,
    )
```

```python
import functools
import math

import jax
import jax.numpy as jnp
from jax import lax
from jax.experimental import pallas as pl
from jax.experimental.pallas import tpu as pltpu
from jax.sharding import PartitionSpec as P

HD = 128
ROT = 32
LOWEST = -1e30
VMEM_LIMIT = 24 << 20
LATE_LIMIT = 24 << 20
ROTARY_LIMIT = 60 << 20


def vmem():
    return pl.BlockSpec(memory_space=pltpu.VMEM)


def smem():
    return pl.BlockSpec(memory_space=pltpu.SMEM)


def column_of(row, size):
    rows = lax.broadcasted_iota(jnp.int32, (size, size), 0)
    cols = lax.broadcasted_iota(jnp.int32, (size, size), 1)
    spread = jnp.broadcast_to(row, (size, size))
    return jnp.sum(jnp.where(rows == cols, spread, 0.0), axis=1, keepdims=True)


def rotary_kernel(
    page,
    segments_ref,
    owners_ref,
    query_ref,
    kv_ref,
    all_kv_ref,
    pool_ref,
    column_ref,
    rot_query_ref,
    rot_key_ref,
    value_ref,
    held_ref,
    cache_ref,
    done,
):
    copies = [
        pltpu.make_async_copy(all_kv_ref.at[1], value_ref, done.at[0]),
        pltpu.make_async_copy(pool_ref, held_ref, done.at[1]),
    ]
    for copy in copies:
        copy.start()
    tokens, feature = query_ref.shape
    segments = segments_ref[...].astype(jnp.float32)
    column = column_of(segments, tokens)
    column_ref[...] = jnp.broadcast_to(column, column_ref.shape)
    earlier = jnp.sum(jnp.where(segments < column, 1.0, 0.0), axis=1, keepdims=True)
    owners = owners_ref[...].astype(jnp.float32)
    cached = jnp.sum(jnp.where(owners == column, 1.0, 0.0), axis=1, keepdims=True)
    number = lax.broadcasted_iota(jnp.int32, (tokens, 1), 0).astype(jnp.float32)
    positions = page * cached + number - earlier
    half = ROT // 2
    lane = lax.broadcasted_iota(jnp.int32, (tokens, HD), 1)
    pair = (lane % half).astype(jnp.float32)
    angles = positions * jnp.exp(-math.log(10000.0) * (2.0 * pair / ROT))
    cosine, sine = jnp.cos(angles), jnp.sin(angles)
    keep = jnp.where(lane < ROT, cosine, 1.0)
    from_above = jnp.where(lane < half, -sine, 0.0)
    from_below = jnp.where((lane >= half) & (lane < ROT), sine, 0.0)
    for start in range(0, feature, HD):
        for source, target in ((kv_ref.at[0], rot_key_ref), (query_ref, rot_query_ref)):
            values = source[:, start : start + HD].astype(jnp.float32)
            turned = (
                values * keep
                + pltpu.roll(values, HD - half, 1) * from_above
                + pltpu.roll(values, half, 1) * from_below
            )
            target[:, start : start + HD] = turned.astype(jnp.bfloat16)
    copies.append(pltpu.make_async_copy(rot_key_ref, cache_ref, done.at[2]))
    copies[-1].start()
    for copy in copies:
        copy.wait()


def anywhere():
    return pl.BlockSpec(memory_space=pltpu.HBM)


def cheap():
    return pl.CostEstimate(flops=1, bytes_accessed=1, transcendentals=0)


def rotate(page, segment_ids, page_owner, queries, new_kv, kv_pool):
    tokens, feature = queries.shape
    shape = jax.ShapeDtypeStruct((tokens, feature), jnp.bfloat16)
    return pl.pallas_call(
        functools.partial(rotary_kernel, page),
        out_shape=(
            jax.ShapeDtypeStruct((tokens, HD), jnp.float32),
            shape,
            shape,
            shape,
            jax.ShapeDtypeStruct(kv_pool.shape, jnp.bfloat16),
            shape,
        ),
        grid=(1,),
        in_specs=[
            pl.BlockSpec(segment_ids.shape, lambda i: (0, 0)),
            pl.BlockSpec(page_owner.shape, lambda i: (0, 0)),
            pl.BlockSpec((tokens, feature), lambda i: (0, 0)),
            pl.BlockSpec((1, tokens, feature), lambda i: (0, 0, 0)),
            anywhere(),
            anywhere(),
        ],
        out_specs=(vmem(),) * 5 + (anywhere(),),
        scratch_shapes=[pltpu.SemaphoreType.DMA((3,))],
        compiler_params=params(ROTARY_LIMIT),
        cost_estimate=cheap(),
        name="rotary",
    )(segment_ids, page_owner, queries, new_kv, new_kv, kv_pool)


def stage_kernel(source_ref, target_ref, done):
    pieces = done.shape[0]
    rows = source_ref.shape[0] // pieces
    copies = []
    for piece in range(pieces):
        part = pl.ds(piece * rows, rows)
        copies.append(
            pltpu.make_async_copy(source_ref.at[part], target_ref.at[part], done.at[piece])
        )
        copies[-1].start()
    for copy in copies:
        copy.wait()


def stage(values):
    return pl.pallas_call(
        stage_kernel,
        out_shape=jax.ShapeDtypeStruct(values.shape, values.dtype),
        in_specs=[pl.BlockSpec(memory_space=pl.ANY)],
        out_specs=vmem(),
        scratch_shapes=[pltpu.SemaphoreType.DMA((8,))],
        compiler_params=params(),
        cost_estimate=cheap(),
        name="stage",
    )(values)


def gather_pages(blocks, refs, per_peer, table_ref, keys, values):
    group = lax.axis_index("dp")
    groups = lax.axis_size("dp")
    page = refs[0].shape[2]
    length = len(blocks) * per_peer * page
    place = lax.broadcasted_iota(jnp.int32, (1, length), 1) // page
    key_owner = jnp.full((1, length), -1, jnp.int32)
    used = 0
    for index, (shift, flip, cuts) in enumerate(blocks):
        holder = lax.rem(group + (4 * shift) % groups, groups) ^ flip
        parts = refs[used : used + len(cuts)]
        used += len(cuts)
        for slot in range(per_peer):
            piece = index * per_peer + slot
            held = table_ref[holder * per_peer + slot]
            rows = pl.ds(piece * page, page)
            for part, low in zip(parts, cuts):
                count = part.shape[0]

                def take(part=part, low=low, count=count):
                    at = jnp.clip(held - low, 0, count - 1)
                    keys[rows, :] = part[at, 0]
                    values[rows, :] = part[at, 1]

                if len(cuts) == 1:
                    take()
                else:
                    pl.when((held >= low) & (held < low + count))(take)
            key_owner = jnp.where(
                place == piece, table_ref[(groups + holder) * per_peer + slot], key_owner
            )
    return key_owner.astype(jnp.float32)


FACTOR = math.log2(math.e) / math.sqrt(HD)
CONTRACT = (((1,), (1,)), ((), ()))


def scores_of(query, keys, seen):
    scores = lax.dot_general(query, keys, CONTRACT, preferred_element_type=jnp.float32)
    return jnp.where(seen, scores * FACTOR, LOWEST)


def weigh(weights, values):
    both = jnp.concatenate([values, jnp.ones_like(values)], axis=1)
    return jnp.dot(weights.astype(jnp.bfloat16), both, preferred_element_type=jnp.float32)


def early_kernel(
    blocks, per_peer, table_ref, segments_ref, column_ref, query_ref, key_ref, value_ref, *refs
):
    *block_refs, mixed_ref, tops_ref, keys, values = refs
    tokens, feature = query_ref.shape
    key_owner = gather_pages(blocks, block_refs, per_peer, table_ref, keys, values)
    segments = segments_ref[...].astype(jnp.float32)
    column = column_ref[:, :1]
    rows = lax.broadcasted_iota(jnp.int32, (tokens, tokens), 0)
    cols = lax.broadcasted_iota(jnp.int32, (tokens, tokens), 1)
    see_new = (column == segments) & (cols <= rows)
    see_old = column == key_owner
    heads = [slice(start, start + HD) for start in range(0, feature, HD)]
    new = [scores_of(query_ref[:, head], key_ref[:, head], see_new) for head in heads]
    old = [scores_of(query_ref[:, head], keys[:, head], see_old) for head in heads]
    peaks = [
        jnp.maximum(jnp.max(a, axis=1, keepdims=True), jnp.max(b, axis=1, keepdims=True))
        for a, b in zip(new, old)
    ]
    new = [jnp.exp2(a - top) for a, top in zip(new, peaks)]
    old = [jnp.exp2(b - top) for b, top in zip(old, peaks)]
    for number, head in enumerate(heads):
        pair = slice(2 * head.start, 2 * head.stop)
        mixed_ref[:, pair] = weigh(new[number], value_ref[:, head]) + weigh(
            old[number], values[:, head]
        )
        tops_ref[:, head] = jnp.broadcast_to(peaks[number], (tokens, HD))


def late_kernel(
    blocks,
    per_peer,
    peers,
    table_ref,
    column_ref,
    query_ref,
    mixed_ref,
    tops_ref,
    weight_ref,
    *refs,
):
    count = sum(len(cuts) for _, _, cuts in blocks)
    block_refs = refs[:count]
    context_ref, own_ref, *send_refs = refs[count : count + 1 + peers]
    keys, values, product = refs[count + 1 + peers :]
    tokens, feature = query_ref.shape
    key_owner = gather_pages(blocks, block_refs, per_peer, table_ref, keys, values)
    seen = column_ref[:, :1] == key_owner
    heads = [slice(start, start + HD) for start in range(0, feature, HD)]
    scores = [scores_of(query_ref[:, head], keys[:, head], seen) for head in heads]
    before = [tops_ref[:, head] for head in heads]
    tops = [
        jnp.maximum(old, jnp.max(new, axis=1, keepdims=True)) for old, new in zip(before, scores)
    ]
    repeat = scores[0].shape[1] // HD
    weights = [
        jnp.exp2(new - jnp.concatenate([top] * repeat, axis=1)) for new, top in zip(scores, tops)
    ]
    fades = [jnp.exp2(old - top) for old, top in zip(before, tops)]
    added = [weigh(part, values[:, head]) for part, head in zip(weights, heads)]
    for number, head in enumerate(heads):
        pair = 2 * head.start
        total = mixed_ref[:, pair + HD : pair + 2 * HD] * fades[number] + added[number][:, HD:]
        mixed = mixed_ref[:, pair : pair + HD] * fades[number] + added[number][:, :HD]
        context_ref[:, head] = (mixed / total).astype(jnp.bfloat16)
    project_rows(peers, 0, context_ref, weight_ref, product, own_ref, send_refs)


def project_rows(peers, first, context_ref, weight_ref, product, own_ref, send_refs):
    rows, width = own_ref.shape
    me = lax.axis_index("tensor")
    step = 256
    for start in range(0, width, step):
        product[:, start : start + step] = jnp.dot(
            context_ref[...],
            weight_ref[:, first + start : first + start + step],
            preferred_element_type=jnp.float32,
        ).astype(jnp.bfloat16)
    own_ref[...] = product[pl.ds(pl.multiple_of(me * rows, rows), rows), :]
    for shift in range(1, peers):
        other = lax.rem(me + shift, peers)
        send_refs[shift - 1][...] = product[pl.ds(pl.multiple_of(other * rows, rows), rows), :]


def shares(tokens, peers, width):
    return (jax.ShapeDtypeStruct((tokens // peers, width), jnp.bfloat16),) * peers


def params(limit=VMEM_LIMIT):
    return pltpu.CompilerParams(vmem_limit_bytes=limit)


def attend_early(layout, table, segment_ids, column, rot_query, rot_key, value, parts, per_peer):
    tokens, feature = rot_query.shape
    prefix = len(layout) * per_peer * parts[0].shape[2]
    return pl.pallas_call(
        functools.partial(early_kernel, layout, per_peer),
        out_shape=(
            jax.ShapeDtypeStruct((tokens, 2 * feature), jnp.float32),
            jax.ShapeDtypeStruct((tokens, feature), jnp.float32),
        ),
        grid=(1,),
        in_specs=[smem()] + [vmem()] * (5 + len(parts)),
        out_specs=(vmem(), vmem()),
        scratch_shapes=[pltpu.VMEM((prefix, feature), jnp.bfloat16)] * 2,
        compiler_params=params(),
        cost_estimate=cheap(),
        name="early",
    )(table, segment_ids, column, rot_query, rot_key, value, *parts)


def attend_late(
    layout, table, column, rot_query, mixed, tops, weight, parts, per_peer, peers, width
):
    tokens, feature = rot_query.shape
    prefix = len(layout) * per_peer * parts[0].shape[2]
    return pl.pallas_call(
        functools.partial(late_kernel, layout, per_peer, peers),
        out_shape=(jax.ShapeDtypeStruct((tokens, feature), jnp.bfloat16),)
        + shares(tokens, peers, width),
        grid=(1,),
        in_specs=[smem()] + [vmem()] * (5 + len(parts)),
        out_specs=(vmem(),) * (1 + peers),
        scratch_shapes=[pltpu.VMEM((prefix, feature), jnp.bfloat16)] * 2
        + [pltpu.VMEM((tokens, width), jnp.bfloat16)],
        compiler_params=params(LATE_LIMIT),
        cost_estimate=cheap(),
        name="late",
    )(table, column, rot_query, mixed, tops, weight, *parts)


def project_kernel(peers, first, context_ref, weight_ref, own_ref, *refs):
    *send_refs, product = refs
    project_rows(peers, first, context_ref, weight_ref, product, own_ref, send_refs)


def project(context, weight, peers, first, width):
    tokens, feature = context.shape
    return pl.pallas_call(
        functools.partial(project_kernel, peers, first),
        out_shape=shares(tokens, peers, width),
        in_specs=[vmem()] * 2,
        out_specs=(vmem(),) * peers,
        scratch_shapes=[pltpu.VMEM((tokens, width), jnp.bfloat16)],
        compiler_params=params(),
        cost_estimate=cheap(),
        name="project",
    )(context, weight)


def base_kernel(residual_ref, bias_ref, *refs):
    *own_refs, base_ref = refs
    start = 0
    for own_ref in own_refs:
        columns = slice(start, start + own_ref.shape[1])
        start += own_ref.shape[1]
        base_ref[:, columns] = (
            residual_ref[:, columns].astype(jnp.float32)
            + own_ref[...].astype(jnp.float32)
            + bias_ref[:, columns].astype(jnp.float32)
        )


def base_of(residual, bias, owns):
    return pl.pallas_call(
        base_kernel,
        out_shape=jax.ShapeDtypeStruct(residual.shape, jnp.float32),
        in_specs=[vmem()] * (2 + len(owns)),
        out_specs=vmem(),
        compiler_params=params(),
        cost_estimate=cheap(),
        name="base",
    )(residual, bias, *owns)


def finish_kernel(first, count, base_ref, *refs):
    received = refs[:count]
    hidden_ref, rounded, done = refs[-3:]
    width = rounded.shape[1]
    step = 256
    copies = []
    for piece in range(width // step):
        start = piece * step
        total = base_ref[:, first + start : first + start + step]
        for part in received:
            total = total + part[:, start : start + step].astype(jnp.float32)
        rounded[:, start : start + step] = total.astype(jnp.bfloat16)
        copies.append(
            pltpu.make_async_copy(
                rounded.at[:, start : start + step],
                hidden_ref.at[:, first + start : first + start + step],
                done.at[piece],
            )
        )
        copies[-1].start()
    for copy in copies:
        copy.wait()


def finish(base, received, first, hidden):
    rows, width = received[0].shape
    before = [] if hidden is None else [hidden]
    return pl.pallas_call(
        functools.partial(finish_kernel, first, len(received)),
        out_shape=jax.ShapeDtypeStruct(base.shape, jnp.bfloat16),
        in_specs=[vmem()] * (1 + len(received)) + [anywhere()] * len(before),
        out_specs=anywhere(),
        scratch_shapes=[
            pltpu.VMEM((rows, width), jnp.bfloat16),
            pltpu.SemaphoreType.DMA((width // 256,)),
        ],
        input_output_aliases={1 + len(received): 0} if before else {},
        compiler_params=params(),
        cost_estimate=cheap(),
        name="finish",
    )(base, *received, *before)


def body(
    residual, queries, new_kv, kv_pool, fetch_pages, page_owner, segment_ids, out_weight, out_bias
):
    group = lax.axis_index("dp")
    groups = lax.axis_size("dp")
    peers = lax.axis_size("tensor")
    per_peer = fetch_pages.shape[2]
    page = kv_pool.shape[2]
    planes = groups // 4
    reach = planes // 2

    def along(values, shift):
        pairs = [(d, (d + 4 * shift) % groups) for d in range(groups)]
        return lax.ppermute(values, "dp", pairs)

    def across(values):
        return lax.ppermute(values, "dp", [(d, d ^ 2) for d in range(groups)])

    def beside(values):
        return lax.ppermute(values, "dp", [(d, d ^ 1) for d in range(groups)])

    wanted = lax.dynamic_index_in_dim(fetch_pages, group, axis=0, keepdims=False).reshape(-1)
    table = jnp.concatenate([wanted, page_owner.reshape(-1)])
    wide = out_weight.shape[1] // 16
    widths = (5 * wide, 4 * wide, 4 * wide, 3 * wide)
    after = lax.optimization_barrier
    ups = {0: kv_pool, 1: along(kv_pool, 1), -1: along(kv_pool, -1)}
    over = {0: across(kv_pool)}
    column, rot_query, rot_key, value, pool, key_cache = rotate(page, segment_ids, page_owner, queries, new_kv, kv_pool)
    ups[1], column = after((ups[1], column))
    for step in range(2, reach):
        ups[step] = along(ups[step - 1], 1)
        ups[-step] = along(ups[1 - step], -1)
    ups[reach] = along(ups[reach - 1], 1)
    first, over[0], out_weight = after((ups[1], over[0], out_weight))
    over[1] = across(first)
    weight = stage(out_weight)
    ups[-1], weight, table = after((ups[-1], weight, table))
    for step in range(2, reach):
        over[step] = across(ups[step])
    for step in range(1, reach):
        over[-step] = across(ups[-step])
    last = min(over)
    crossed, near = over[reach - 1], over[last]
    crossed, ups[reach] = after((crossed, ups[reach]))

    layout, parts, rest = [], [], []
    for flip, found in ((0, ups), (2, over)):
        for shift, values in found.items():
            if (flip, shift) in ((0, reach), (2, reach - 1)):
                rest.append((shift, flip, values))
            elif (flip, shift) != (2, last):
                layout += [(-shift, flip, (0,)), (-shift, flip ^ 1, (0,))]
                parts += [pool if values is kv_pool else values, beside(values)]
    mixed, tops = attend_early(
        layout, table, segment_ids, column, rot_query, rot_key, value, parts, per_peer
    )
    far = along(crossed, 1)
    near, mixed = after((near, mixed))
    far, mixed = after((far, mixed))
    rest += [(last, 2, near), (reach, 2, far)]
    layout, parts = [], []
    for shift, flip, values in rest:
        layout += [(-shift, flip, (0,)), (-shift, flip ^ 1, (0,))]
        parts += [values, beside(values)]
    context, *share = attend_late(
        layout, table, column, rot_query, mixed, tops, weight, parts, per_peer, peers, widths[0]
    )
    owns, received = [share[0]], []
    start = 0
    for number, width in enumerate(widths):
        pieces = []
        for shift, values in enumerate(share[1:], 1):
            pairs = [(t, (t + shift) % peers) for t in range(peers)]
            pieces.append(lax.ppermute(values, "tensor", pairs))
        received.append(pieces)
        start += width
        if number + 1 < len(widths):
            share = project(context, weight, peers, start, widths[number + 1])
            owns.append(share[0])
    base = base_of(residual, out_bias.reshape(1, -1), owns)
    hidden, start = None, 0
    for width, pieces in zip(widths, received):
        hidden = finish(base, pieces, start, hidden)
        start += width
    return (hidden, key_cache)


def solution(mesh):
    return jax.shard_map(
        body,
        mesh=mesh,
        in_specs=(
            P(("dp", "tensor"), None),
            P("dp", "tensor"),
            P(None, "dp", "tensor"),
            P("dp", None, None, "tensor"),
            P(),
            P("dp", None),
            P("dp", None),
            P("tensor", None),
            P(),
        ),
        out_specs=(P(("dp", "tensor"), None), P("dp", "tensor")),
        check_vma=False,
    )
```

```python
import functools
import math

import jax
import jax.numpy as jnp
from jax import lax
from jax.experimental import pallas as pl
from jax.experimental.pallas import tpu as pltpu
from jax.sharding import PartitionSpec as P

HD = 128
ROT = 32
LOWEST = -1e30
VMEM_LIMIT = 24 << 20
LATE_LIMIT = 24 << 20
ROTARY_LIMIT = 60 << 20


def vmem():
    return pl.BlockSpec(memory_space=pltpu.VMEM)


def smem():
    return pl.BlockSpec(memory_space=pltpu.SMEM)


def column_of(row, size):
    rows = lax.broadcasted_iota(jnp.int32, (size, size), 0)
    cols = lax.broadcasted_iota(jnp.int32, (size, size), 1)
    spread = jnp.broadcast_to(row, (size, size))
    return jnp.sum(jnp.where(rows == cols, spread, 0.0), axis=1, keepdims=True)


def rotary_kernel(
    page,
    segments_ref,
    owners_ref,
    query_ref,
    kv_ref,
    all_kv_ref,
    pool_ref,
    column_ref,
    rot_query_ref,
    rot_key_ref,
    value_ref,
    held_ref,
    cache_ref,
    done,
):
    copies = [
        pltpu.make_async_copy(all_kv_ref.at[1], value_ref, done.at[0]),
        pltpu.make_async_copy(pool_ref, held_ref, done.at[1]),
    ]
    for copy in copies:
        copy.start()
    tokens, feature = query_ref.shape
    segments = segments_ref[...].astype(jnp.float32)
    column = column_of(segments, tokens)
    column_ref[...] = jnp.broadcast_to(column, column_ref.shape)
    earlier = jnp.sum(jnp.where(segments < column, 1.0, 0.0), axis=1, keepdims=True)
    owners = owners_ref[...].astype(jnp.float32)
    cached = jnp.sum(jnp.where(owners == column, 1.0, 0.0), axis=1, keepdims=True)
    number = lax.broadcasted_iota(jnp.int32, (tokens, 1), 0).astype(jnp.float32)
    positions = page * cached + number - earlier
    half = ROT // 2
    lane = lax.broadcasted_iota(jnp.int32, (tokens, HD), 1)
    pair = (lane % half).astype(jnp.float32)
    angles = positions * jnp.exp(-math.log(10000.0) * (2.0 * pair / ROT))
    cosine, sine = jnp.cos(angles), jnp.sin(angles)
    keep = jnp.where(lane < ROT, cosine, 1.0)
    from_above = jnp.where(lane < half, -sine, 0.0)
    from_below = jnp.where((lane >= half) & (lane < ROT), sine, 0.0)
    for start in range(0, feature, HD):
        for source, target in ((kv_ref.at[0], rot_key_ref), (query_ref, rot_query_ref)):
            values = source[:, start : start + HD].astype(jnp.float32)
            turned = (
                values * keep
                + pltpu.roll(values, HD - half, 1) * from_above
                + pltpu.roll(values, half, 1) * from_below
            )
            target[:, start : start + HD] = turned.astype(jnp.bfloat16)
    copies.append(pltpu.make_async_copy(rot_key_ref, cache_ref, done.at[2]))
    copies[-1].start()
    for copy in copies:
        copy.wait()


def anywhere():
    return pl.BlockSpec(memory_space=pltpu.HBM)


def cheap():
    return pl.CostEstimate(flops=1, bytes_accessed=1, transcendentals=0)


def rotate(page, segment_ids, page_owner, queries, new_kv, kv_pool):
    tokens, feature = queries.shape
    shape = jax.ShapeDtypeStruct((tokens, feature), jnp.bfloat16)
    return pl.pallas_call(
        functools.partial(rotary_kernel, page),
        out_shape=(
            jax.ShapeDtypeStruct((tokens, HD), jnp.float32),
            shape,
            shape,
            shape,
            jax.ShapeDtypeStruct(kv_pool.shape, jnp.bfloat16),
            shape,
        ),
        grid=(1,),
        in_specs=[
            pl.BlockSpec(segment_ids.shape, lambda i: (0, 0)),
            pl.BlockSpec(page_owner.shape, lambda i: (0, 0)),
            pl.BlockSpec((tokens, feature), lambda i: (0, 0)),
            pl.BlockSpec((1, tokens, feature), lambda i: (0, 0, 0)),
            anywhere(),
            anywhere(),
        ],
        out_specs=(vmem(),) * 5 + (anywhere(),),
        scratch_shapes=[pltpu.SemaphoreType.DMA((3,))],
        compiler_params=params(ROTARY_LIMIT),
        cost_estimate=cheap(),
        name="rotary",
    )(segment_ids, page_owner, queries, new_kv, new_kv, kv_pool)


def stage_kernel(source_ref, target_ref, done):
    pieces = done.shape[0]
    rows = source_ref.shape[0] // pieces
    copies = []
    for piece in range(pieces):
        part = pl.ds(piece * rows, rows)
        copies.append(
            pltpu.make_async_copy(source_ref.at[part], target_ref.at[part], done.at[piece])
        )
        copies[-1].start()
    for copy in copies:
        copy.wait()


def stage(values):
    return pl.pallas_call(
        stage_kernel,
        out_shape=jax.ShapeDtypeStruct(values.shape, values.dtype),
        in_specs=[pl.BlockSpec(memory_space=pl.ANY)],
        out_specs=vmem(),
        scratch_shapes=[pltpu.SemaphoreType.DMA((8,))],
        compiler_params=params(),
        cost_estimate=cheap(),
        name="stage",
    )(values)


def gather_pages(blocks, refs, per_peer, table_ref, keys, values):
    group = lax.axis_index("dp")
    groups = lax.axis_size("dp")
    page = refs[0].shape[2]
    length = len(blocks) * per_peer * page
    place = lax.broadcasted_iota(jnp.int32, (1, length), 1) // page
    key_owner = jnp.full((1, length), -1, jnp.int32)
    used = 0
    for index, (shift, flip, cuts) in enumerate(blocks):
        holder = lax.rem(group + (4 * shift) % groups, groups) ^ flip
        parts = refs[used : used + len(cuts)]
        used += len(cuts)
        for slot in range(per_peer):
            piece = index * per_peer + slot
            held = table_ref[holder * per_peer + slot]
            rows = pl.ds(piece * page, page)
            for part, low in zip(parts, cuts):
                count = part.shape[0]

                def take(part=part, low=low, count=count):
                    at = jnp.clip(held - low, 0, count - 1)
                    keys[rows, :] = part[at, 0]
                    values[rows, :] = part[at, 1]

                if len(cuts) == 1:
                    take()
                else:
                    pl.when((held >= low) & (held < low + count))(take)
            key_owner = jnp.where(
                place == piece, table_ref[(groups + holder) * per_peer + slot], key_owner
            )
    return key_owner.astype(jnp.float32)


FACTOR = math.log2(math.e) / math.sqrt(HD)
CONTRACT = (((1,), (1,)), ((), ()))


def scores_of(query, keys, seen):
    scores = lax.dot_general(query, keys, CONTRACT, preferred_element_type=jnp.float32)
    return jnp.where(seen, scores * FACTOR, LOWEST)


def weigh(weights, values):
    both = jnp.concatenate([values, jnp.ones_like(values)], axis=1)
    return jnp.dot(weights.astype(jnp.bfloat16), both, preferred_element_type=jnp.float32)


def early_kernel(
    blocks, per_peer, table_ref, segments_ref, column_ref, query_ref, key_ref, value_ref, *refs
):
    *block_refs, mixed_ref, tops_ref, keys, values = refs
    tokens, feature = query_ref.shape
    key_owner = gather_pages(blocks, block_refs, per_peer, table_ref, keys, values)
    segments = segments_ref[...].astype(jnp.float32)
    column = column_ref[:, :1]
    rows = lax.broadcasted_iota(jnp.int32, (tokens, tokens), 0)
    cols = lax.broadcasted_iota(jnp.int32, (tokens, tokens), 1)
    see_new = (column == segments) & (cols <= rows)
    see_old = column == key_owner
    heads = [slice(start, start + HD) for start in range(0, feature, HD)]
    new = [scores_of(query_ref[:, head], key_ref[:, head], see_new) for head in heads]
    old = [scores_of(query_ref[:, head], keys[:, head], see_old) for head in heads]
    peaks = [
        jnp.maximum(jnp.max(a, axis=1, keepdims=True), jnp.max(b, axis=1, keepdims=True))
        for a, b in zip(new, old)
    ]
    new = [jnp.exp2(a - top) for a, top in zip(new, peaks)]
    old = [jnp.exp2(b - top) for b, top in zip(old, peaks)]
    for number, head in enumerate(heads):
        pair = slice(2 * head.start, 2 * head.stop)
        mixed_ref[:, pair] = weigh(new[number], value_ref[:, head]) + weigh(
            old[number], values[:, head]
        )
        tops_ref[:, head] = jnp.broadcast_to(peaks[number], (tokens, HD))


def late_kernel(
    blocks,
    per_peer,
    peers,
    table_ref,
    column_ref,
    query_ref,
    mixed_ref,
    tops_ref,
    weight_ref,
    *refs,
):
    count = sum(len(cuts) for _, _, cuts in blocks)
    block_refs = refs[:count]
    context_ref, own_ref, *send_refs = refs[count : count + 1 + peers]
    keys, values, product = refs[count + 1 + peers :]
    tokens, feature = query_ref.shape
    key_owner = gather_pages(blocks, block_refs, per_peer, table_ref, keys, values)
    seen = column_ref[:, :1] == key_owner
    heads = [slice(start, start + HD) for start in range(0, feature, HD)]
    scores = [scores_of(query_ref[:, head], keys[:, head], seen) for head in heads]
    before = [tops_ref[:, head] for head in heads]
    tops = [
        jnp.maximum(old, jnp.max(new, axis=1, keepdims=True)) for old, new in zip(before, scores)
    ]
    repeat = scores[0].shape[1] // HD
    weights = [
        jnp.exp2(new - jnp.concatenate([top] * repeat, axis=1)) for new, top in zip(scores, tops)
    ]
    fades = [jnp.exp2(old - top) for old, top in zip(before, tops)]
    added = [weigh(part, values[:, head]) for part, head in zip(weights, heads)]
    for number, head in enumerate(heads):
        pair = 2 * head.start
        total = mixed_ref[:, pair + HD : pair + 2 * HD] * fades[number] + added[number][:, HD:]
        mixed = mixed_ref[:, pair : pair + HD] * fades[number] + added[number][:, :HD]
        context_ref[:, head] = (mixed / total).astype(jnp.bfloat16)
    project_rows(peers, 0, context_ref, weight_ref, product, own_ref, send_refs)


def project_rows(peers, first, context_ref, weight_ref, product, own_ref, send_refs):
    rows, width = own_ref.shape
    me = lax.axis_index("tensor")
    step = 256
    for start in range(0, width, step):
        product[:, start : start + step] = jnp.dot(
            context_ref[...],
            weight_ref[:, first + start : first + start + step],
            preferred_element_type=jnp.float32,
        ).astype(jnp.bfloat16)
    own_ref[...] = product[pl.ds(pl.multiple_of(me * rows, rows), rows), :]
    for shift in range(1, peers):
        other = lax.rem(me + shift, peers)
        send_refs[shift - 1][...] = product[pl.ds(pl.multiple_of(other * rows, rows), rows), :]


def shares(tokens, peers, width):
    return (jax.ShapeDtypeStruct((tokens // peers, width), jnp.bfloat16),) * peers


def params(limit=VMEM_LIMIT):
    return pltpu.CompilerParams(vmem_limit_bytes=limit)


def attend_early(layout, table, segment_ids, column, rot_query, rot_key, value, parts, per_peer):
    tokens, feature = rot_query.shape
    prefix = len(layout) * per_peer * parts[0].shape[2]
    return pl.pallas_call(
        functools.partial(early_kernel, layout, per_peer),
        out_shape=(
            jax.ShapeDtypeStruct((tokens, 2 * feature), jnp.float32),
            jax.ShapeDtypeStruct((tokens, feature), jnp.float32),
        ),
        grid=(1,),
        in_specs=[smem()] + [vmem()] * (5 + len(parts)),
        out_specs=(vmem(), vmem()),
        scratch_shapes=[pltpu.VMEM((prefix, feature), jnp.bfloat16)] * 2,
        compiler_params=params(),
        cost_estimate=cheap(),
        name="early",
    )(table, segment_ids, column, rot_query, rot_key, value, *parts)


def attend_late(
    layout, table, column, rot_query, mixed, tops, weight, parts, per_peer, peers, width
):
    tokens, feature = rot_query.shape
    prefix = len(layout) * per_peer * parts[0].shape[2]
    return pl.pallas_call(
        functools.partial(late_kernel, layout, per_peer, peers),
        out_shape=(jax.ShapeDtypeStruct((tokens, feature), jnp.bfloat16),)
        + shares(tokens, peers, width),
        grid=(1,),
        in_specs=[smem()] + [vmem()] * (5 + len(parts)),
        out_specs=(vmem(),) * (1 + peers),
        scratch_shapes=[pltpu.VMEM((prefix, feature), jnp.bfloat16)] * 2
        + [pltpu.VMEM((tokens, width), jnp.bfloat16)],
        compiler_params=params(LATE_LIMIT),
        cost_estimate=cheap(),
        name="late",
    )(table, column, rot_query, mixed, tops, weight, *parts)


def project_kernel(peers, first, context_ref, weight_ref, own_ref, *refs):
    *send_refs, product = refs
    project_rows(peers, first, context_ref, weight_ref, product, own_ref, send_refs)


def project(context, weight, peers, first, width):
    tokens, feature = context.shape
    return pl.pallas_call(
        functools.partial(project_kernel, peers, first),
        out_shape=shares(tokens, peers, width),
        in_specs=[vmem()] * 2,
        out_specs=(vmem(),) * peers,
        scratch_shapes=[pltpu.VMEM((tokens, width), jnp.bfloat16)],
        compiler_params=params(),
        cost_estimate=cheap(),
        name="project",
    )(context, weight)


def base_kernel(residual_ref, bias_ref, *refs):
    *own_refs, base_ref = refs
    start = 0
    for own_ref in own_refs:
        columns = slice(start, start + own_ref.shape[1])
        start += own_ref.shape[1]
        base_ref[:, columns] = (
            residual_ref[:, columns].astype(jnp.float32)
            + own_ref[...].astype(jnp.float32)
            + bias_ref[:, columns].astype(jnp.float32)
        )


def base_of(residual, bias, owns):
    return pl.pallas_call(
        base_kernel,
        out_shape=jax.ShapeDtypeStruct(residual.shape, jnp.float32),
        in_specs=[vmem()] * (2 + len(owns)),
        out_specs=vmem(),
        compiler_params=params(),
        cost_estimate=cheap(),
        name="base",
    )(residual, bias, *owns)


def finish_kernel(first, count, base_ref, *refs):
    received = refs[:count]
    hidden_ref, rounded, done = refs[-3:]
    width = rounded.shape[1]
    step = 256
    copies = []
    for piece in range(width // step):
        start = piece * step
        total = base_ref[:, first + start : first + start + step]
        for part in received:
            total = total + part[:, start : start + step].astype(jnp.float32)
        rounded[:, start : start + step] = total.astype(jnp.bfloat16)
        copies.append(
            pltpu.make_async_copy(
                rounded.at[:, start : start + step],
                hidden_ref.at[:, first + start : first + start + step],
                done.at[piece],
            )
        )
        copies[-1].start()
    for copy in copies:
        copy.wait()


def finish(base, received, first, hidden):
    rows, width = received[0].shape
    before = [] if hidden is None else [hidden]
    return pl.pallas_call(
        functools.partial(finish_kernel, first, len(received)),
        out_shape=jax.ShapeDtypeStruct(base.shape, jnp.bfloat16),
        in_specs=[vmem()] * (1 + len(received)) + [anywhere()] * len(before),
        out_specs=anywhere(),
        scratch_shapes=[
            pltpu.VMEM((rows, width), jnp.bfloat16),
            pltpu.SemaphoreType.DMA((width // 256,)),
        ],
        input_output_aliases={1 + len(received): 0} if before else {},
        compiler_params=params(),
        cost_estimate=cheap(),
        name="finish",
    )(base, *received, *before)


def body(
    residual, queries, new_kv, kv_pool, fetch_pages, page_owner, segment_ids, out_weight, out_bias
):
    group = lax.axis_index("dp")
    groups = lax.axis_size("dp")
    peers = lax.axis_size("tensor")
    per_peer = fetch_pages.shape[2]
    page = kv_pool.shape[2]
    planes = groups // 4
    reach = planes // 2

    def along(values, shift):
        pairs = [(d, (d + 4 * shift) % groups) for d in range(groups)]
        return lax.ppermute(values, "dp", pairs)

    def across(values):
        return lax.ppermute(values, "dp", [(d, d ^ 2) for d in range(groups)])

    def beside(values):
        return lax.ppermute(values, "dp", [(d, d ^ 1) for d in range(groups)])

    wanted = lax.dynamic_index_in_dim(fetch_pages, group, axis=0, keepdims=False).reshape(-1)
    table = jnp.concatenate([wanted, page_owner.reshape(-1)])
    wide = out_weight.shape[1] // 16
    widths = (6 * wide, 5 * wide, 3 * wide, 2 * wide)
    after = lax.optimization_barrier
    ups = {0: kv_pool, 1: along(kv_pool, 1), -1: along(kv_pool, -1)}
    over = {0: across(kv_pool)}
    column, rot_query, rot_key, value, pool, key_cache = rotate(page, segment_ids, page_owner, queries, new_kv, kv_pool)
    ups[1], column = after((ups[1], column))
    for step in range(2, reach):
        ups[step] = along(ups[step - 1], 1)
        ups[-step] = along(ups[1 - step], -1)
    ups[reach] = along(ups[reach - 1], 1)
    first, over[0], out_weight = after((ups[1], over[0], out_weight))
    over[1] = across(first)
    weight = stage(out_weight)
    ups[-1], weight, table = after((ups[-1], weight, table))
    for step in range(2, reach):
        over[step] = across(ups[step])
    for step in range(1, reach):
        over[-step] = across(ups[-step])
    last = min(over)
    crossed, near = over[reach - 1], over[last]
    crossed, ups[reach] = after((crossed, ups[reach]))

    layout, parts, rest = [], [], []
    for flip, found in ((0, ups), (2, over)):
        for shift, values in found.items():
            if (flip, shift) in ((0, reach), (2, reach - 1)):
                rest.append((shift, flip, values))
            elif (flip, shift) != (2, last):
                layout += [(-shift, flip, (0,)), (-shift, flip ^ 1, (0,))]
                parts += [pool if values is kv_pool else values, beside(values)]
    mixed, tops = attend_early(
        layout, table, segment_ids, column, rot_query, rot_key, value, parts, per_peer
    )
    far = along(crossed, 1)
    near, mixed = after((near, mixed))
    far, mixed = after((far, mixed))
    rest += [(last, 2, near), (reach, 2, far)]
    layout, parts = [], []
    for shift, flip, values in rest:
        layout += [(-shift, flip, (0,)), (-shift, flip ^ 1, (0,))]
        parts += [values, beside(values)]
    context, *share = attend_late(
        layout, table, column, rot_query, mixed, tops, weight, parts, per_peer, peers, widths[0]
    )
    owns, received = [share[0]], []
    start = 0
    for number, width in enumerate(widths):
        pieces = []
        for shift, values in enumerate(share[1:], 1):
            pairs = [(t, (t + shift) % peers) for t in range(peers)]
            pieces.append(lax.ppermute(values, "tensor", pairs))
        received.append(pieces)
        start += width
        if number + 1 < len(widths):
            share = project(context, weight, peers, start, widths[number + 1])
            owns.append(share[0])
    base = base_of(residual, out_bias.reshape(1, -1), owns)
    hidden, start = None, 0
    for width, pieces in zip(widths, received):
        hidden = finish(base, pieces, start, hidden)
        start += width
    return (hidden, key_cache)


def solution(mesh):
    return jax.shard_map(
        body,
        mesh=mesh,
        in_specs=(
            P(("dp", "tensor"), None),
            P("dp", "tensor"),
            P(None, "dp", "tensor"),
            P("dp", None, None, "tensor"),
            P(),
            P("dp", None),
            P("dp", None),
            P("tensor", None),
            P(),
        ),
        out_specs=(P(("dp", "tensor"), None), P("dp", "tensor")),
        check_vma=False,
    )
```
